32 devices in a mesh: ctx: 8 (over y, x, core), ch: 4 (over z).
Axes of the slice: x: 2, y: 2, z: 4, core: 2. Of those that a mesh axis runs over, the one named last changes fastest.
Arguments:
- query_one: bfloat16 [1024, 4096], P('ch', 'ctx'), may hold values from -6 to 6
- key_one: bfloat16 [1024, 4096], P('ch', 'ctx'), may hold values from -6 to 6
- value_one: bfloat16 [1024, 4096], P('ch', 'ctx'), may hold values from -6 to 6
- query_two: bfloat16 [1024, 4096], P('ch', 'ctx'), may hold values from -6 to 6
- key_two: bfloat16 [1024, 4096], P('ch', 'ctx'), may hold values from -6 to 6
- out_grad: bfloat16 [1024, 4096], P('ch', 'ctx'), may hold values from -6 to 6
- mr_filter: bfloat16 [64, 128], P('ch'), may hold values from -0.5 to 0.5
- li_rate: float32 [64, 16], P('ch'), may hold values from 3.6621094e-05 to 0.055
- li_residue: float32 [64, 16], P('ch'), may hold values from -1.5 to 1.5
- out_weight: bfloat16 [1024, 1024], P('ch'), may hold values from -0.1875 to 0.1875
Outputs:
- mixed: bfloat16 [1024, 4096], P('ch', 'ctx')
- query_one_grad: bfloat16 [1024, 4096], P('ch', 'ctx')
- key_one_grad: bfloat16 [1024, 4096], P('ch', 'ctx')
- value_one_grad: bfloat16 [1024, 4096], P('ch', 'ctx')
- query_two_grad: bfloat16 [1024, 4096], P('ch', 'ctx')
- key_two_grad: bfloat16 [1024, 4096], P('ch', 'ctx')
- weight_grad: float32 [1024, 1024], P('ch')
- filter_grad: float32 [64, 128], P('ch')
The draws below stay inside these ranges and needn't reach their ends.
All inputs are finite; a program needn't handle non-finite values.
Results may differ from the reference program's by a relative error of at most 0.015.
Values may be sent and summed in bfloat16 or wider, within the bound.
No kernel may reach another device: no remote copies, remote signals or barrier semaphores. Data moves between devices by JAX's collectives and lax.ppermute only.
A program may use at most 128 MiB of HBM per device.

```python
import math
import jax
import jax.numpy as jnp
from jax import lax

GROUPS = 64
TAPS = 128
MODES = 16
L_DEV = 512
TOKENS = 4096
CHANNELS = 1024


def draw_li_rate(key, part):
    pick_key, slow_key, fast_key = jax.random.split(key, 3)
    portion = 0.5
    layout_shape = (GROUPS, MODES)
    slow_mask = jax.random.uniform(pick_key, layout_shape, jnp.float32) < portion
    slow_rate = jnp.exp(jax.random.uniform(slow_key, layout_shape, jnp.float32, math.log(0.2 / TOKENS), math.log(2.3 / TOKENS)))
    fast_rate = jnp.exp(jax.random.uniform(fast_key, layout_shape, jnp.float32, math.log(1.0 / L_DEV), math.log(0.05)))
    chosen = jnp.where(slow_mask, slow_rate, fast_rate)
    return jnp.clip(chosen, 0.15 / TOKENS, 0.055)


def shard_levels(stream_key, shape, pieces, low, top_value):
    factor_of, own = 1.0, jax.random.fold_in(stream_key, 6)
    for dim, shards_of in pieces:
        draws = jnp.exp(jax.random.uniform(jax.random.fold_in(own, dim), (shards_of,), jnp.float32, low / len(pieces), top_value / len(pieces)))
        factor_of = factor_of * jnp.repeat(draws, shape[dim] // shards_of).reshape([-1 if axis == dim else 1 for axis in range(len(shape))])
    return factor_of


def normal_values(rng, extent, scale, bound, cuts=(), kind=jnp.bfloat16):
    gain = shard_levels(rng, extent, cuts, -0.22, 0.18) if cuts else 1.0
    entries = jax.random.normal(rng, extent, jnp.float32) * scale * gain
    return jnp.minimum(jnp.maximum(entries, -bound), bound).astype(kind)


def setup_inputs(seed: int = 0) -> dict:
    seeds = jax.random.split(jax.random.key(seed), 11)
    query_one = normal_values(seeds[0], (CHANNELS, TOKENS), 1.0, 6.0, ((0, 4), (1, 8)))
    key_one = normal_values(seeds[1], (CHANNELS, TOKENS), 1.0, 6.0, ((0, 4), (1, 8)))
    value_one = normal_values(seeds[2], (CHANNELS, TOKENS), 1.0, 6.0, ((0, 4), (1, 8)))
    query_two = normal_values(seeds[3], (CHANNELS, TOKENS), 1.0, 6.0, ((0, 4), (1, 8)))
    key_two = normal_values(seeds[4], (CHANNELS, TOKENS), 1.0, 6.0, ((0, 4), (1, 8)))
    out_grad = normal_values(seeds[5], (CHANNELS, TOKENS), 1.0, 6.0, ((0, 4), (1, 8)))
    mr_filter = normal_values(seeds[6], (GROUPS, TAPS), TAPS ** -0.5, 0.5, ((0, 4),))
    li_rate = draw_li_rate(jax.random.fold_in(seeds[10], 71), 0)
    li_residue = normal_values(seeds[8], (GROUPS, MODES), 0.25, 1.5, ((0, 4),), jnp.float32)
    out_weight = normal_values(seeds[9], (CHANNELS, CHANNELS), CHANNELS ** -0.5, 0.1875, ((0, 4),))
    return dict(query_one=query_one, key_one=key_one, value_one=value_one, query_two=query_two, key_two=key_two, out_grad=out_grad, mr_filter=mr_filter, li_rate=li_rate, li_residue=li_residue, out_weight=out_weight)


highest_precision = lax.Precision.HIGHEST

def short_matrices(taps_row):
    tap_count = taps_row.shape[1]
    row_index = jnp.arange(tap_count)[:, None]
    col_index = jnp.arange(tap_count)[None, :]
    lag_inside = row_index - col_index
    lag_before = lag_inside + tap_count
    zero_value = jnp.zeros((), taps_row.dtype)
    inside = jnp.where(lag_inside >= 0, taps_row[:, jnp.clip(lag_inside, 0, tap_count - 1)], zero_value)
    before = jnp.where(lag_before < tap_count, taps_row[:, jnp.clip(lag_before, 0, tap_count - 1)], zero_value)
    return (inside, before)

def short_conv(stream, taps_row):
    group_count, tap_count = taps_row.shape
    chan_count, length = stream.shape
    inside, before = short_matrices(taps_row)
    blocks = stream.reshape(group_count, chan_count // group_count, length // tap_count, tap_count)
    earlier = jnp.concatenate([jnp.zeros_like(blocks[:, :, :1]), blocks[:, :, :-1]], axis=2)
    result = jnp.einsum('gij,gcbj->gcbi', inside, blocks, precision=highest_precision)
    result = result + jnp.einsum('gij,gcbj->gcbi', before, earlier, precision=highest_precision)
    return result.reshape(chan_count, length)

def short_conv_back(grad_rows, taps_row):
    group_count, tap_count = taps_row.shape
    chan_count, length = grad_rows.shape
    inside, before = short_matrices(taps_row)
    blocks = grad_rows.reshape(group_count, chan_count // group_count, length // tap_count, tap_count)
    later_blocks = jnp.concatenate([blocks[:, :, 1:], jnp.zeros_like(blocks[:, :, :1])], axis=2)
    result = jnp.einsum('gji,gcbj->gcbi', inside, blocks, precision=highest_precision)
    result = result + jnp.einsum('gji,gcbj->gcbi', before, later_blocks, precision=highest_precision)
    return result.reshape(chan_count, length)

def long_conv(stream, decay_rate, residue):
    chan_count, length = stream.shape
    group_count = decay_rate.shape[0]
    mode_coef = residue * jnp.sqrt(-jnp.expm1(-2.0 * decay_rate))
    offsets = jnp.arange(length).astype(decay_rate.dtype)
    padded_len = 2 * length

    def per_group(inputs):
        rows_in, group_rate, group_coef = inputs
        kernel = lax.optimization_barrier(jnp.sum(group_coef[:, None] * jnp.exp(-group_rate[:, None] * offsets[None, :]), axis=0))
        spectrum = jnp.fft.rfft(rows_in, padded_len, axis=-1) * jnp.fft.rfft(kernel, padded_len)[None, :]
        return jnp.fft.irfft(spectrum, padded_len, axis=-1)[:, :length]
    result = lax.map(per_group, (stream.reshape(group_count, chan_count // group_count, length), decay_rate, mode_coef))
    return result.reshape(chan_count, length)

def reference(query_one, key_one, value_one, query_two, key_two, out_grad, mr_filter, li_rate, li_residue, out_weight):
    chan_count, length = query_one.shape
    product_one = (key_one.astype(jnp.float32) * value_one.astype(jnp.float32)).astype(jnp.bfloat16)
    taps_float = mr_filter.astype(jnp.float32)
    product_float = product_one.astype(jnp.float32)
    conv_one = short_conv(product_float, taps_float)
    gated_one = (query_one.astype(jnp.float32) * conv_one).astype(jnp.bfloat16)
    product_two = (key_two.astype(jnp.float32) * gated_one.astype(jnp.float32)).astype(jnp.bfloat16)
    conv_two = long_conv(product_two.astype(jnp.float32), li_rate, li_residue).astype(jnp.bfloat16)
    gated_two = (query_two.astype(jnp.float32) * conv_two.astype(jnp.float32)).astype(jnp.bfloat16)
    mixed = jnp.dot(out_weight.T, gated_two, preferred_element_type=jnp.float32).astype(jnp.bfloat16)
    grad_scale = 1.0 / math.sqrt(TOKENS)
    gated_two_grad = jnp.dot(out_weight, out_grad, preferred_element_type=jnp.float32)
    weight_grad = grad_scale * jnp.dot(gated_two, out_grad.T, preferred_element_type=jnp.float32)
    query_two_grad = (gated_two_grad * conv_two.astype(jnp.float32)).astype(jnp.bfloat16)
    conv_two_grad = (gated_two_grad * query_two.astype(jnp.float32)).astype(jnp.bfloat16)
    flipped = jnp.flip(conv_two_grad.astype(jnp.float32), axis=1)
    product_two_grad = jnp.flip(long_conv(flipped, li_rate, li_residue), axis=1).astype(jnp.bfloat16)
    key_two_grad = (product_two_grad.astype(jnp.float32) * gated_one.astype(jnp.float32)).astype(jnp.bfloat16)
    gated_one_grad = product_two_grad.astype(jnp.float32) * key_two.astype(jnp.float32)
    query_one_grad = (gated_one_grad * conv_one).astype(jnp.bfloat16)
    conv_one_grad = (gated_one_grad * query_one.astype(jnp.float32)).astype(jnp.bfloat16)
    product_one_grad = short_conv_back(conv_one_grad.astype(jnp.float32), taps_float)
    key_one_grad = (product_one_grad * value_one.astype(jnp.float32)).astype(jnp.bfloat16)
    value_one_grad = (product_one_grad * key_one.astype(jnp.float32)).astype(jnp.bfloat16)

    def conv_of(taps_row):
        return short_conv(product_float, taps_row)
    pullback = jax.vjp(conv_of, taps_float)[1]
    filter_grad = grad_scale * pullback(conv_one_grad.astype(jnp.float32))[0]
    return (mixed, query_one_grad, key_one_grad, value_one_grad, query_two_grad, key_two_grad, weight_grad, filter_grad)
```

```python
import functools
import math

import jax
import jax.numpy as jnp
from jax import lax
from jax.experimental import pallas as pl
from jax.experimental.pallas import tpu as pltpu
from jax.sharding import PartitionSpec as P

BLK = 128
HIGHEST = lax.Precision.HIGHEST
F32 = jnp.float32
BF16 = jnp.bfloat16


def dot(a, b, ca=1, cb=0, precision=None):
    return lax.dot_general(
        a, b, (((ca,), (cb,)), ((), ())), preferred_element_type=F32, precision=precision
    )


def split(x):
    hi = x.astype(BF16)
    return hi, (x - hi.astype(F32)).astype(BF16)


def iota(shape, dim):
    return lax.broadcasted_iota(jnp.int32, shape, dim)


def rows_of(ref, g, size, first, count):
    return jnp.concatenate(
        [
            ref[g * size : (g + 1) * size, (first + b) * BLK : (first + b + 1) * BLK]
            for b in range(count)
        ],
        axis=0,
    )


def put_rows(ref, g, size, value):
    for b in range(value.shape[0] // size):
        ref[g * size : (g + 1) * size, b * BLK : (b + 1) * BLK] = value[
            b * size : (b + 1) * size
        ].astype(ref.dtype)


def circulant(row):
    return pltpu.roll(jnp.broadcast_to(row, (BLK, BLK)), 0, 1, stride=1, stride_axis=0)


def per_channel(table, size):
    groups = table.shape[0]
    chans = groups * size
    pick = (iota((groups, chans), 1) // size == iota((groups, chans), 0)).astype(F32)
    return dot(table, pick, 0, 0, HIGHEST)


def block_states(table, stream, groups, modes, size):
    half = groups * modes
    chans = groups * size
    full = dot(table, stream, 1, 1)
    full = full[:half] + full[half:]
    own = iota((half, chans), 0) // modes == iota((half, chans), 1) // size
    return jnp.sum(jnp.where(own, full, 0.0).reshape(groups, modes, chans), axis=0)


def state_terms(states, table, groups, modes, size):
    chans = groups * size
    half = groups * modes
    count = len(states)
    hi, lo = split(jnp.concatenate(states, axis=1))
    pick = (iota((modes, half), 1) % modes == iota((modes, half), 0)).astype(BF16)
    own = (iota((count * chans, half), 0) % chans) // size == iota((count * chans, half), 1) // modes
    wide_hi = jnp.where(own, dot(hi, pick, 0, 0), 0.0).astype(BF16)
    wide_lo = jnp.where(own, dot(lo, pick, 0, 0), 0.0).astype(BF16)
    out = dot(jnp.concatenate([wide_hi, wide_lo, wide_hi], axis=1), table)
    return [out[i * chans : (i + 1) * chans] for i in range(count)]


def tables_kernel(size, taps, rate, coef, short, long, close, open_, reach, meet, rate_t, coef_t):
    groups, modes = rate.shape
    half = groups * modes
    wide_rate = jnp.broadcast_to(rate[...][:, None, :], (groups, modes, modes)).reshape(half, modes)
    diag = iota((half, modes), 0) % modes == iota((half, modes), 1)
    col = jnp.sum(jnp.where(diag, wide_rate, 0.0), axis=1, keepdims=True)
    wide_coef = jnp.broadcast_to(coef[...][:, None, :], (groups, modes, modes)).reshape(half, modes)
    coef_col = jnp.sum(jnp.where(diag, wide_coef, 0.0), axis=1, keepdims=True)
    at = iota((half, BLK), 1).astype(F32)
    falling = jnp.exp(-col * at)
    hi, lo = split(falling)
    open_[0:half] = hi
    open_[half:] = lo
    hi, lo = split(jnp.exp(-col * (BLK - 1.0 - at)))
    close[0:half] = hi
    close[half:] = lo
    hi, lo = split(jnp.exp(-col * (at + 1.0)))
    reach[0:half] = hi
    reach[half : 2 * half] = hi
    reach[2 * half :] = lo
    hi, lo = split(jnp.exp(-col * (BLK - at)))
    meet[0:half] = hi
    meet[half : 2 * half] = hi
    meet[2 * half :] = lo
    kernel = jnp.sum((coef_col * falling).reshape(groups, modes, BLK), axis=1)
    tap_rows = taps[...].astype(F32)
    later = iota((BLK, BLK), 1) >= iota((BLK, BLK), 0)
    for g in range(groups):
        turned = circulant(tap_rows[g : g + 1])
        short[g, 0:BLK] = jnp.where(later, 0.0, turned).astype(BF16)
        short[g, BLK:] = jnp.where(later, turned, 0.0).astype(BF16)
        long[g] = jnp.where(later, circulant(kernel[g : g + 1]), 0.0).astype(BF16)
    rate_t[...] = per_channel(rate[...], size)
    coef_t[...] = per_channel(coef[...], size)


def first_kernel(
    size, halo, q1, k1, v1, k2, short, long, close, rate_t, conv, gated, local, sub, sent, stream
):
    groups = short.shape[0]
    modes = rate_t.shape[0]
    count = q1.shape[1] // BLK
    for g in range(groups):
        rows = slice(g * size, (g + 1) * size)
        p1 = (rows_of(k1, g, size, 0, count).astype(F32) * rows_of(v1, g, size, 0, count).astype(F32)).astype(BF16)
        before = jnp.concatenate([halo[rows], p1[: (count - 1) * size]], axis=0)
        c1 = dot(jnp.concatenate([before, p1], axis=1), short[g])
        put_rows(conv, g, size, c1)
        g1 = (rows_of(q1, g, size, 0, count).astype(F32) * c1).astype(BF16)
        put_rows(gated, g, size, g1)
        p2 = (rows_of(k2, g, size, 0, count).astype(F32) * g1.astype(F32)).astype(BF16)
        put_rows(stream, g, size, p2)
        put_rows(local, g, size, dot(p2, long[g]))
    decay = jnp.exp(-rate_t[...] * BLK)
    total = None
    for b in range(count):
        state = block_states(close[...], stream[:, b * BLK : (b + 1) * BLK], groups, modes, size)
        sub[b] = state
        total = state if total is None else total * decay + state
    for d in range(sent.shape[0]):
        sent[d] = total


def second_kernel(
    size, groups, states, sub, rate_t, coef_t, reach, local, q2, weight, conv2, gated2, *parts
):
    modes = rate_t.shape[0]
    ctx_size, count = states.shape[0], sub.shape[0]
    length = float(count * BLK)
    me = lax.axis_index("ctx")
    rate = rate_t[...]
    entering = jnp.zeros(rate.shape, F32)
    for d in range(ctx_size):
        gap = me - 1 - d
        factor = jnp.exp(-rate * (length * jnp.maximum(gap, 0).astype(F32)))
        entering = entering + jnp.where(gap >= 0, factor * states[d], 0.0)
    decay = jnp.exp(-rate * BLK)
    coefs = coef_t[...]
    all_states = []
    for b in range(count):
        all_states.append(coefs * entering)
        entering = decay * entering + sub[b]
    terms = state_terms(all_states, reach[...], groups, modes, size)
    for b in range(count):
        cols = slice(b * BLK, (b + 1) * BLK)
        c2 = (local[:, cols].astype(F32) + terms[b]).astype(BF16)
        conv2[:, cols] = c2
        gated2[:, cols] = (q2[:, cols].astype(F32) * c2.astype(F32)).astype(BF16)
    here = lax.axis_index("ch")
    width = weight.shape[1] // len(parts)
    for k, part in enumerate(parts):
        at = pl.multiple_of(lax.rem(here + k, len(parts)) * width, BLK)
        part[...] = dot(weight[:, pl.ds(at, width)], gated2[...], 0, 0).astype(BF16)


def third_kernel(size, n_ch, fused, *refs):
    grads = refs[:n_ch]
    (weight, q2, k2, q1, conv2, gated2, long, open_, meet, rate_t, coef_t) = refs[n_ch : n_ch + 11]
    (q2_grad, local, sub, edge, sent, wsent, stream) = refs[n_ch + 11 :]
    groups = long.shape[0]
    modes, chans = rate_t.shape
    length = q2.shape[1]
    count = length // BLK
    here = lax.axis_index("ch")
    width = weight.shape[1] // n_ch
    starts = [
        pl.multiple_of(lax.rem(here - k + n_ch, n_ch) * width, BLK) for k in range(n_ch)
    ]
    acc = None
    for k in range(n_ch):
        term = dot(weight[:, pl.ds(starts[k], width)], grads[k][...])
        acc = term if acc is None else acc + term
    q2_grad[...] = (acc * conv2[...].astype(F32)).astype(BF16)
    stream[...] = (acc * q2[...].astype(F32)).astype(BF16)
    for g in range(groups):
        put_rows(local, g, size, dot(rows_of(stream, g, size, 0, count), long[g], 1, 1))
    decay = jnp.exp(-rate_t[...] * BLK)
    total, inner = None, None
    for b in reversed(range(count)):
        state = block_states(open_[...], stream[:, b * BLK : (b + 1) * BLK], groups, modes, size)
        sub[b] = state
        inner = total
        total = state if total is None else total * decay + state
    (term,) = state_terms([coef_t[...] * inner], meet[...], groups, modes, size)
    edge[:, :BLK] = (local[:, :BLK].astype(F32) + term).astype(BF16)
    edge[:, BLK:] = (k2[:, :BLK].astype(F32) * q1[:, :BLK].astype(F32)).astype(BF16)
    if fused:
        rows = chans // sent.shape[0]
        hi, lo = split(total)
        for d in range(sent.shape[0]):
            sent[d, rows:, 0:chans] = hi
            sent[d, rows:, chans : 2 * chans] = lo
            sent[d, rows:, 2 * chans :] = jnp.zeros((modes, sent.shape[2] - 2 * chans), BF16)
        wsent[...] = jnp.zeros(wsent.shape, wsent.dtype)
    else:
        for d in range(sent.shape[0]):
            sent[d] = total
    for k in range(n_ch):
        part = dot(gated2[...], grads[k][...], 1, 1)
        if fused:
            part = part.astype(BF16)
            for d in range(sent.shape[0]):
                sent[d, 0:rows, pl.ds(starts[k], width)] = part[d * rows : (d + 1) * rows]
        else:
            wsent[:, pl.ds(starts[k], width)] = part


def fourth_kernel(size, fused, *refs):
    (states, edge, sub, rate_t, coef_t, meet, local, q1, k1, v1, k2, conv, gated, halo, short) = refs[:15]
    (k2_grad, q1_grad, k1_grad, v1_grad, out, stream) = refs[15:]
    groups = short.shape[0]
    modes, chans = rate_t.shape
    count = sub.shape[0]
    length = float(count * BLK)
    ctx_size = states.shape[0]
    me = lax.axis_index("ctx")
    rate = rate_t[...]
    coefs = coef_t[...]
    beyond = jnp.zeros(rate.shape, F32)
    following = jnp.zeros(rate.shape, F32)
    for d in range(ctx_size):
        if fused:
            rows = chans // ctx_size
            state = states[d, rows:, 0:chans].astype(F32) + states[d, rows:, chans : 2 * chans].astype(F32)
        else:
            state = states[d]
        gap = d - me - 2
        factor = jnp.exp(-rate * (length * jnp.maximum(gap, 0).astype(F32)))
        beyond = beyond + jnp.where(gap >= 0, factor * state, 0.0)
        following = following + jnp.where(gap == -1, state, 0.0)
    decay = jnp.exp(-rate * BLK)
    entering = jnp.exp(-rate * length) * beyond + following
    all_states = [coefs * (jnp.exp(-rate * (length - BLK)) * beyond)]
    for b in reversed(range(count)):
        all_states.append(coefs * entering)
        entering = decay * entering + sub[b]
    terms = state_terms(all_states, meet[...], groups, modes, size)
    next_p = (edge[:, :BLK].astype(F32) + terms[0]).astype(BF16)
    stream[:, count * BLK :] = (next_p.astype(F32) * edge[:, BLK:].astype(F32)).astype(BF16)
    for b in range(count):
        cols = slice(b * BLK, (b + 1) * BLK)
        p2g = (local[:, cols].astype(F32) + terms[count - b]).astype(BF16).astype(F32)
        k2_grad[:, cols] = (p2g * gated[:, cols].astype(F32)).astype(BF16)
        g1g = p2g * k2[:, cols].astype(F32)
        q1_grad[:, cols] = (g1g * conv[:, cols].astype(F32)).astype(BF16)
        stream[:, cols] = (g1g * q1[:, cols].astype(F32)).astype(BF16)
    across_sum = iota((BLK, BLK), 1) + iota((BLK, BLK), 0)
    later = across_sum >= BLK - 1
    mirror = (across_sum == BLK - 1).astype(BF16)
    filters = []
    for g in range(groups):
        rows_g = slice(g * size, (g + 1) * size)
        kv, vv = rows_of(k1, g, size, 0, count).astype(F32), rows_of(v1, g, size, 0, count).astype(F32)
        p1 = (kv * vv).astype(BF16)
        here = rows_of(stream, g, size, 0, count)
        after = rows_of(stream, g, size, 1, count)
        p1g = dot(here, short[g, BLK:], 1, 1) + dot(after, short[g, 0:BLK], 1, 1)
        put_rows(k1_grad, g, size, p1g * vv)
        put_rows(v1_grad, g, size, p1g * kv)
        seen = dot(jnp.concatenate([halo[rows_g], p1], axis=0), mirror).astype(BF16)
        inside = dot(seen[size:], here, 0, 0)
        across = dot(seen[: count * size], here, 0, 0)
        both = jnp.where(later, inside, across)
        turned = pltpu.roll(both, 1, 1, stride=1, stride_axis=0)
        filters.append(jnp.sum(turned, axis=0, keepdims=True))
    filter_rows = jnp.concatenate(filters, axis=0)
    if fused:
        total = states[0, 0:rows].astype(F32)
        for d in range(1, ctx_size):
            total = total + states[d, 0:rows].astype(F32)
        total = total.astype(BF16)
        hi, lo = split(filter_rows)
        for d in range(ctx_size):
            out[d, 0:rows] = total
            out[d, rows:, 0:BLK] = hi
            out[d, rows:, BLK : 2 * BLK] = lo
            out[d, rows:, 2 * BLK :] = jnp.zeros((modes, out.shape[2] - 2 * BLK), BF16)
    else:
        out[...] = filter_rows


def call(kernel, outs, *args, scratch=(), flops=0, name=None):
    size = sum(math.prod(a.shape) * a.dtype.itemsize for a in args)
    size += sum(math.prod(s) * jnp.dtype(t).itemsize for s, t in outs)
    return pl.pallas_call(
        kernel,
        out_shape=[jax.ShapeDtypeStruct(s, t) for s, t in outs],
        scratch_shapes=list(scratch),
        cost_estimate=pl.CostEstimate(flops=flops, bytes_accessed=size, transcendentals=0),
        name=name,
    )(*args)


def around(count, step):
    return [(i, (i + step) % count) for i in range(count)]


def on_device(q1, k1, v1, q2, k2, out_grad, taps, rate, residue, weight):
    chans, length = q1.shape
    groups, tap_count = taps.shape
    modes = rate.shape[1]
    size = chans // groups
    half = groups * modes
    count = length // BLK
    n_ctx, n_ch = lax.axis_size("ctx"), lax.axis_size("ch")
    rows = chans // n_ctx
    fused = rows % 16 == 0 and groups == modes
    out_chans = weight.shape[1]
    width = out_chans // n_ch

    tail = (k1[:, length - BLK :].astype(F32) * v1[:, length - BLK :].astype(F32)).astype(BF16)
    halo = lax.ppermute(tail, "ctx", [(i, i + 1) for i in range(n_ctx - 1)])
    grads = [out_grad] + [lax.ppermute(out_grad, "ch", around(n_ch, k)) for k in range(1, n_ch)]

    coef = residue * jnp.sqrt(-jnp.expm1(-2.0 * rate))
    short, long, close, open_, reach, meet, rate_t, coef_t = call(
        functools.partial(tables_kernel, size),
        [
            ((groups, 2 * BLK, BLK), BF16),
            ((groups, BLK, BLK), BF16),
            ((2 * half, BLK), BF16),
            ((2 * half, BLK), BF16),
            ((3 * half, BLK), BF16),
            ((3 * half, BLK), BF16),
            ((modes, chans), F32),
            ((modes, chans), F32),
        ],
        taps,
        rate,
        coef,
        name="tables",
    )
    stream = [((chans, length), BF16)]
    conv, gated, local, sub, sent = call(
        functools.partial(first_kernel, size),
        stream * 3 + [((count, modes, chans), F32), ((n_ctx, modes, chans), F32)],
        halo,
        q1,
        k1,
        v1,
        k2,
        short,
        long,
        close,
        rate_t,
        scratch=[pltpu.VMEM((chans, length), BF16)],
        name="first",
    )
    states = lax.all_to_all(sent, "ctx", 0, 0, tiled=True)
    conv2, gated2, *parts = call(
        functools.partial(second_kernel, size, groups),
        stream * 2 + [((width, length), BF16)] * n_ch,
        states,
        sub,
        rate_t,
        coef_t,
        reach,
        local,
        q2,
        weight,
        name="second",
    )
    mixed_parts = [parts[0]] + [
        lax.ppermute(parts[k], "ch", around(n_ch, k)) for k in range(1, n_ch)
    ]
    if fused:
        sent_shape, spare = ((n_ctx, rows + modes, out_chans), BF16), ((8, BLK), F32)
    else:
        sent_shape, spare = ((n_ctx, modes, chans), F32), ((chans, out_chans), F32)
    q2_grad, local_back, sub_back, edge, sent_back, weight_part = call(
        functools.partial(third_kernel, size, n_ch, fused),
        stream * 2 + [((count, modes, chans), F32), ((chans, 2 * BLK), BF16), sent_shape, spare],
        *grads,
        weight,
        q2,
        k2,
        q1,
        conv2,
        gated2,
        long,
        open_,
        meet,
        rate_t,
        coef_t,
        scratch=[pltpu.VMEM((chans, length), BF16)],
        name="third",
    )
    next_edge = lax.ppermute(edge, "ctx", [(i + 1, i) for i in range(n_ctx - 1)])
    states_back = lax.all_to_all(sent_back, "ctx", 0, 0, tiled=True)
    last_shape = sent_shape if fused else ((groups, BLK), F32)
    k2_grad, q1_grad, k1_grad, v1_grad, last = call(
        functools.partial(fourth_kernel, size, fused),
        stream * 4 + [last_shape],
        states_back,
        next_edge,
        sub_back,
        rate_t,
        coef_t,
        meet,
        local_back,
        q1,
        k1,
        v1,
        k2,
        conv,
        gated,
        halo,
        short,
        scratch=[pltpu.VMEM((chans, length + BLK), BF16)],
        name="fourth",
    )
    scale = 1.0 / math.sqrt(length * n_ctx)
    if fused:
        final = lax.all_to_all(last, "ctx", 0, 0, tiled=True)
        weight_grad = scale * final[:, :rows].astype(F32).reshape(chans, out_chans)
        pieces = final[:, rows:, : 2 * BLK].astype(F32)
        filter_grad = scale * jnp.sum(pieces[:, :, :BLK] + pieces[:, :, BLK:], axis=0)
    else:
        weight_total, filter_total = lax.psum((weight_part, last), "ctx")
        weight_grad = scale * weight_total
        filter_grad = scale * filter_total
    mixed = sum(p.astype(F32) for p in mixed_parts).astype(BF16)
    return (mixed, q1_grad, k1_grad, v1_grad, q2_grad, k2_grad, weight_grad, filter_grad)


def solution(mesh):
    cut, rows_only = P("ch", "ctx"), P("ch", None)
    return jax.shard_map(
        on_device,
        mesh=mesh,
        in_specs=(cut,) * 6 + (rows_only,) * 4,
        out_specs=(cut,) * 6 + (rows_only,) * 2,
        check_vma=False,
    )
```

```python
import functools
import math

import jax
import jax.numpy as jnp
from jax import lax
from jax.experimental import pallas as pl
from jax.experimental.pallas import tpu as pltpu
from jax.sharding import PartitionSpec as P

BLK = 128
VMEM_LIMIT = 12 << 20
HIGHEST = lax.Precision.HIGHEST
F32 = jnp.float32
BF16 = jnp.bfloat16


def dot(a, b, ca=1, cb=0, precision=None):
    return lax.dot_general(
        a, b, (((ca,), (cb,)), ((), ())), preferred_element_type=F32, precision=precision
    )


def split(x):
    hi = x.astype(BF16)
    return hi, (x - hi.astype(F32)).astype(BF16)


def iota(shape, dim):
    return lax.broadcasted_iota(jnp.int32, shape, dim)


def rows_of(ref, g, size, first, count):
    return jnp.concatenate(
        [
            ref[g * size : (g + 1) * size, (first + b) * BLK : (first + b + 1) * BLK]
            for b in range(count)
        ],
        axis=0,
    )


def put_rows(ref, g, size, value):
    for b in range(value.shape[0] // size):
        ref[g * size : (g + 1) * size, b * BLK : (b + 1) * BLK] = value[
            b * size : (b + 1) * size
        ].astype(ref.dtype)


def circulant(row):
    return pltpu.roll(jnp.broadcast_to(row, (BLK, BLK)), 0, 1, stride=1, stride_axis=0)


def column(table):
    groups, modes = table.shape
    wide = jnp.broadcast_to(table[:, None, :], (groups, modes, modes)).reshape(-1, modes)
    diag = iota(wide.shape, 0) % modes == iota(wide.shape, 1)
    return jnp.sum(jnp.where(diag, wide, 0.0), axis=1, keepdims=True)


def meeting(rate, groups, modes):
    half = groups * modes
    hi, lo = split(jnp.exp(-column(rate) * (BLK - iota((half, BLK), 1).astype(F32))))
    return jnp.concatenate([hi, hi, lo], axis=0)


def per_channel(table, size):
    groups = table.shape[0]
    chans = groups * size
    pick = (iota((groups, chans), 1) // size == iota((groups, chans), 0)).astype(F32)
    return dot(table, pick, 0, 0, HIGHEST)


def block_states(table, stream, groups, modes, size):
    half = groups * modes
    chans = groups * size
    full = dot(table, stream, 1, 1)
    full = full[:half] + full[half:]
    own = iota((half, chans), 0) // modes == iota((half, chans), 1) // size
    return jnp.sum(jnp.where(own, full, 0.0).reshape(groups, modes, chans), axis=0)


def state_terms(states, table, groups, modes, size):
    chans = groups * size
    half = groups * modes
    count = len(states)
    hi, lo = split(jnp.concatenate(states, axis=1))
    pick = (iota((modes, half), 1) % modes == iota((modes, half), 0)).astype(BF16)
    own = (iota((count * chans, half), 0) % chans) // size == iota((count * chans, half), 1) // modes
    wide_hi = jnp.where(own, dot(hi, pick, 0, 0), 0.0).astype(BF16)
    wide_lo = jnp.where(own, dot(lo, pick, 0, 0), 0.0).astype(BF16)
    out = dot(jnp.concatenate([wide_hi, wide_lo, wide_hi], axis=1), table)
    return [out[i * chans : (i + 1) * chans] for i in range(count)]


def pack_rows(ref, d, first, value, width):
    half = value.shape[0] // 2
    for i, part in enumerate(split(value)):
        for j in range(2):
            at = (2 * i + j) * value.shape[1]
            ref[d, first:, at : at + value.shape[1]] = part[j * half : (j + 1) * half]
    if 4 * value.shape[1] < width:
        ref[d, first:, 4 * value.shape[1] :] = jnp.zeros((half, width - 4 * value.shape[1]), BF16)


def unpack_rows(ref, d, first, width):
    parts = [ref[d, first:, i * width : (i + 1) * width].astype(F32) for i in range(4)]
    return jnp.concatenate([parts[0] + parts[2], parts[1] + parts[3]], axis=0)


def tables_kernel(size, held, *refs):
    taps, rate, coef = refs[:3]
    sources = refs[3 : 3 + held]
    (short, long, close, open_, reach, rate_t, coef_t) = refs[3 + held : 10 + held]
    targets, sems = refs[10 + held : -1], refs[-1]
    copies = [
        pltpu.make_async_copy(source, target, sems.at[i])
        for i, (source, target) in enumerate(zip(sources, targets))
    ]
    for copy in copies:
        copy.start()
    groups, modes = rate.shape
    half = groups * modes
    col, coef_col = column(rate[...]), column(coef[...])
    at = iota((half, BLK), 1).astype(F32)
    falling = jnp.exp(-col * at)
    hi, lo = split(falling)
    open_[0:half] = hi
    open_[half:] = lo
    hi, lo = split(jnp.exp(-col * (BLK - 1.0 - at)))
    close[0:half] = hi
    close[half:] = lo
    hi, lo = split(jnp.exp(-col * (at + 1.0)))
    reach[0:half] = hi
    reach[half : 2 * half] = hi
    reach[2 * half :] = lo
    kernel = jnp.sum((coef_col * falling).reshape(groups, modes, BLK), axis=1)
    tap_rows = taps[...].astype(F32)
    later = iota((BLK, BLK), 1) >= iota((BLK, BLK), 0)
    for g in range(groups):
        turned = circulant(tap_rows[g : g + 1])
        short[g, 0:BLK] = jnp.where(later, 0.0, turned).astype(BF16)
        short[g, BLK:] = jnp.where(later, turned, 0.0).astype(BF16)
        long[g] = jnp.where(later, circulant(kernel[g : g + 1]), 0.0).astype(BF16)
    rate_t[...] = per_channel(rate[...], size)
    coef_t[...] = per_channel(coef[...], size)
    for copy in copies:
        copy.wait()


def first_kernel(
    size,
    halo,
    q1,
    k1,
    v1,
    k2,
    short,
    long,
    close,
    rate_t,
    conv,
    gated,
    local,
    mirrored,
    ahead,
    sub,
    sent,
    stream,
):
    groups = short.shape[0]
    modes = rate_t.shape[0]
    count = q1.shape[1] // BLK
    seen = jnp.where(lax.axis_index("ctx") > 0, halo[...], jnp.zeros(halo.shape, BF16))
    mirror = (iota((BLK, BLK), 1) + iota((BLK, BLK), 0) == BLK - 1).astype(BF16)
    for g in range(groups):
        rows = slice(g * size, (g + 1) * size)
        p1 = (rows_of(k1, g, size, 0, count).astype(F32) * rows_of(v1, g, size, 0, count).astype(F32)).astype(BF16)
        before = jnp.concatenate([seen[rows], p1[: (count - 1) * size]], axis=0)
        c1 = dot(jnp.concatenate([before, p1], axis=1), short[g])
        put_rows(conv, g, size, c1)
        g1 = (rows_of(q1, g, size, 0, count).astype(F32) * c1).astype(BF16)
        put_rows(gated, g, size, g1)
        p2 = (rows_of(k2, g, size, 0, count).astype(F32) * g1.astype(F32)).astype(BF16)
        put_rows(stream, g, size, p2)
        put_rows(local, g, size, dot(p2, long[g]))
    mirrored[:, :BLK] = dot(seen, mirror).astype(BF16)
    ahead[...] = (k2[:, :BLK].astype(F32) * q1[:, :BLK].astype(F32)).astype(BF16)
    for b in range(count):
        cols = slice(b * BLK, (b + 1) * BLK)
        p1 = (k1[:, cols].astype(F32) * v1[:, cols].astype(F32)).astype(BF16)
        mirrored[:, (b + 1) * BLK : (b + 2) * BLK] = dot(p1, mirror).astype(BF16)
    decay = jnp.exp(-rate_t[...] * BLK)
    total = None
    for b in range(count):
        state = block_states(close[...], stream[:, b * BLK : (b + 1) * BLK], groups, modes, size)
        sub[b] = state
        total = state if total is None else total * decay + state
    for d in range(sent.shape[0]):
        sent[d] = total


def second_kernel(
    size, groups, states, sub, rate_t, coef_t, reach, local, q2, weight, conv2, gated2, *parts
):
    modes = rate_t.shape[0]
    ctx_size, count = states.shape[0], sub.shape[0]
    length = float(count * BLK)
    me = lax.axis_index("ctx")
    rate = rate_t[...]
    entering = jnp.zeros(rate.shape, F32)
    for d in range(ctx_size):
        gap = me - 1 - d
        factor = jnp.exp(-rate * (length * jnp.maximum(gap, 0).astype(F32)))
        entering = entering + jnp.where(gap >= 0, factor * states[d], 0.0)
    decay = jnp.exp(-rate * BLK)
    coefs = coef_t[...]
    all_states = []
    for b in range(count):
        all_states.append(coefs * entering)
        entering = decay * entering + sub[b]
    terms = state_terms(all_states, reach[...], groups, modes, size)
    for b in range(count):
        cols = slice(b * BLK, (b + 1) * BLK)
        c2 = (local[:, cols].astype(F32) + terms[b]).astype(BF16)
        conv2[:, cols] = c2
        gated2[:, cols] = (q2[:, cols].astype(F32) * c2.astype(F32)).astype(BF16)
    here = lax.axis_index("ch")
    width = weight.shape[1] // len(parts)
    for k, part in enumerate(parts):
        at = pl.multiple_of(lax.rem(here + k, len(parts)) * width, BLK)
        part[...] = dot(weight[:, pl.ds(at, width)], gated2[...], 0, 0).astype(BF16)


def third_kernel(size, n_ch, fused, *refs):
    grads = refs[:n_ch]
    (weight, q2, conv2, gated2, long, open_, rate_t, coef_t, rate_g, ahead) = refs[n_ch : n_ch + 10]
    (q2_grad, local, sub, edge, sent, wsent, stream) = refs[n_ch + 10 :]
    groups = long.shape[0]
    modes, chans = rate_t.shape
    count = q2.shape[1] // BLK
    here = lax.axis_index("ch")
    width = weight.shape[1] // n_ch
    starts = [
        pl.multiple_of(lax.rem(here - k + n_ch, n_ch) * width, BLK) for k in range(n_ch)
    ]
    acc = None
    for k in range(n_ch):
        term = dot(weight[:, pl.ds(starts[k], width)], grads[k][...])
        acc = term if acc is None else acc + term
    q2_grad[...] = (acc * conv2[...].astype(F32)).astype(BF16)
    stream[...] = (acc * q2[...].astype(F32)).astype(BF16)
    for g in range(groups):
        put_rows(local, g, size, dot(rows_of(stream, g, size, 0, count), long[g], 1, 1))
    decay = jnp.exp(-rate_t[...] * BLK)
    total, inner = None, None
    for b in reversed(range(count)):
        state = block_states(open_[...], stream[:, b * BLK : (b + 1) * BLK], groups, modes, size)
        sub[b] = state
        inner = total
        total = state if total is None else total * decay + state
    meet = meeting(rate_g[...], groups, modes)
    (term,) = state_terms([coef_t[...] * inner], meet, groups, modes, size)
    edge[:, :BLK] = (local[:, :BLK].astype(F32) + term).astype(BF16)
    edge[:, BLK:] = ahead[...]
    if fused:
        rows = chans // sent.shape[0]
        for d in range(sent.shape[0]):
            pack_rows(sent, d, rows, total, sent.shape[2])
        wsent[...] = jnp.zeros(wsent.shape, wsent.dtype)
    else:
        for d in range(sent.shape[0]):
            sent[d] = total
    for k in range(n_ch):
        part = dot(gated2[...], grads[k][...], 1, 1)
        if fused:
            part = part.astype(BF16)
            for d in range(sent.shape[0]):
                sent[d, 0:rows, pl.ds(starts[k], width)] = part[d * rows : (d + 1) * rows]
        else:
            wsent[:, pl.ds(starts[k], width)] = part


def fourth_kernel(size, fused, states, edge, sub, rate_t, coef_t, rate_g, local, q1, k2, mirrored, p2_grad, turned_grad, out):
    modes, chans = rate_t.shape
    groups = chans // size
    count = sub.shape[0]
    length = float(count * BLK)
    ctx_size = states.shape[0]
    rows = chans // ctx_size
    me = lax.axis_index("ctx")
    rate = rate_t[...]
    coefs = coef_t[...]
    beyond = jnp.zeros(rate.shape, F32)
    following = jnp.zeros(rate.shape, F32)
    for d in range(ctx_size):
        if fused:
            state = unpack_rows(states, d, rows, chans)
        else:
            state = states[d]
        gap = d - me - 2
        factor = jnp.exp(-rate * (length * jnp.maximum(gap, 0).astype(F32)))
        beyond = beyond + jnp.where(gap >= 0, factor * state, 0.0)
        following = following + jnp.where(gap == -1, state, 0.0)
    decay = jnp.exp(-rate * BLK)
    entering = jnp.exp(-rate * length) * beyond + following
    all_states = [coefs * (jnp.exp(-rate * (length - BLK)) * beyond)]
    for b in reversed(range(count)):
        all_states.append(coefs * entering)
        entering = decay * entering + sub[b]
    terms = state_terms(all_states, meeting(rate_g[...], groups, modes), groups, modes, size)
    next_p = (edge[:, :BLK].astype(F32) + terms[0]).astype(BF16)
    beside = (next_p.astype(F32) * edge[:, BLK:].astype(F32)).astype(BF16)
    turned_grad[:, count * BLK :] = jnp.where(me < ctx_size - 1, beside, jnp.zeros(beside.shape, BF16))
    for b in range(count):
        cols = slice(b * BLK, (b + 1) * BLK)
        p2g = (local[:, cols].astype(F32) + terms[count - b]).astype(BF16)
        p2_grad[:, cols] = p2g
        g1g = p2g.astype(F32) * k2[:, cols].astype(F32)
        turned_grad[:, cols] = (g1g * q1[:, cols].astype(F32)).astype(BF16)
    later = iota((BLK, BLK), 1) + iota((BLK, BLK), 0) >= BLK - 1
    filters = []
    for g in range(groups):
        here = rows_of(turned_grad, g, size, 0, count)
        seen = rows_of(mirrored, g, size, 0, count + 1)
        inside = dot(seen[size:], here, 0, 0)
        across = dot(seen[: count * size], here, 0, 0)
        turned = pltpu.roll(jnp.where(later, inside, across), 1, 1, stride=1, stride_axis=0)
        filters.append(jnp.sum(turned, axis=0, keepdims=True))
    filter_rows = jnp.concatenate(filters, axis=0)
    if fused:
        total = states[0, 0:rows].astype(F32)
        for d in range(1, ctx_size):
            total = total + states[d, 0:rows].astype(F32)
        total = total.astype(BF16)
        for d in range(ctx_size):
            out[d, 0:rows] = total
            pack_rows(out, d, rows, filter_rows, out.shape[2])
    else:
        out[...] = filter_rows


def fifth_kernel(size, p2_grad, turned_grad, q2_grad, gated, conv, k2, k1, v1, short, q2_out, k2_out, q1_out, k1_out, v1_out):
    groups = short.shape[0]
    count = p2_grad.shape[1] // BLK
    q2_out[...] = q2_grad[...]
    p2g = p2_grad[...].astype(F32)
    k2_out[...] = (p2g * gated[...].astype(F32)).astype(BF16)
    q1_out[...] = (p2g * k2[...].astype(F32) * conv[...].astype(F32)).astype(BF16)
    for g in range(groups):
        kv, vv = rows_of(k1, g, size, 0, count).astype(F32), rows_of(v1, g, size, 0, count).astype(F32)
        here = rows_of(turned_grad, g, size, 0, count)
        after = rows_of(turned_grad, g, size, 1, count)
        p1g = dot(here, short[g, BLK:], 1, 1) + dot(after, short[g, 0:BLK], 1, 1)
        put_rows(k1_out, g, size, p1g * vv)
        put_rows(v1_out, g, size, p1g * kv)


def last_kernel(scale, moved, weight_out, filter_out):
    ctx_size, rows = weight_out.shape[:2]
    total = None
    for d in range(ctx_size):
        weight_out[d] = scale * moved[d, 0:rows].astype(F32)
        term = unpack_rows(moved, d, rows, BLK)
        total = term if total is None else total + term
    filter_out[...] = scale * total


def call(kernel, outs, *args, held=(), scratch=(), name):
    size = sum(math.prod(a.shape) * a.dtype.itemsize for a in args)
    size += sum(math.prod(s) * jnp.dtype(t).itemsize for s, t in outs)
    results = pl.pallas_call(
        kernel,
        out_shape=[
            pltpu.VMEM(s, t) if i in held else pltpu.HBM(s, t) for i, (s, t) in enumerate(outs)
        ],
        in_specs=[
            pl.BlockSpec(memory_space=pltpu.HBM if name == "tables" and i > 2 else pltpu.VMEM)
            for i in range(len(args))
        ],
        out_specs=[pl.BlockSpec(memory_space=pltpu.VMEM)] * len(outs),
        scratch_shapes=list(scratch),
        cost_estimate=pl.CostEstimate(flops=0, bytes_accessed=size, transcendentals=0),
        compiler_params=pltpu.CompilerParams(vmem_limit_bytes=VMEM_LIMIT),
    )(*args)
    return [
        pltpu.with_memory_space_constraint(o, pltpu.VMEM) if i in held else o
        for i, o in enumerate(results)
    ]


def around(count, step):
    return [(i, (i + step) % count) for i in range(count)]


def on_device(q1, k1, v1, q2, k2, out_grad, taps, rate, residue, weight):
    chans, length = q1.shape
    groups, _ = taps.shape
    modes = rate.shape[1]
    size = chans // groups
    half = groups * modes
    count = length // BLK
    n_ctx, n_ch = lax.axis_size("ctx"), lax.axis_size("ch")
    rows = chans // n_ctx
    fused = rows % 16 == 0 and groups == modes == 16 and 4 * chans == weight.shape[1]
    out_chans = weight.shape[1]
    width = out_chans // n_ch

    tail = (k1[:, length - BLK :].astype(F32) * v1[:, length - BLK :].astype(F32)).astype(BF16)
    halo = lax.ppermute(tail, "ctx", around(n_ctx, 1))
    grads = []
    for k in range(1, n_ch):
        grads.append(lax.ppermute(out_grad, "ch", around(n_ch, k)))

    coef = residue * jnp.sqrt(-jnp.expm1(-2.0 * rate))
    loaded = [
        pltpu.with_memory_space_constraint(a, pltpu.HBM)
        for a in (q1, k1, v1, q2, k2, out_grad, weight)
    ]
    late_q1, late_k1, late_v1, _, late_k2 = loaded[:5]
    short, long, close, open_, reach, rate_t, coef_t, q1, k1, v1, q2, k2, out_grad, weight = call(
        functools.partial(tables_kernel, size, len(loaded)),
        [
            ((groups, 2 * BLK, BLK), BF16),
            ((groups, BLK, BLK), BF16),
            ((2 * half, BLK), BF16),
            ((2 * half, BLK), BF16),
            ((3 * half, BLK), BF16),
            ((modes, chans), F32),
            ((modes, chans), F32),
        ]
        + [(a.shape, a.dtype) for a in loaded],
        taps,
        rate,
        coef,
        *loaded,
        held=range(14),
        scratch=[pltpu.SemaphoreType.DMA((len(loaded),))],
        name="tables",
    )
    stream = ((chans, length), BF16)
    blocks = ((count, modes, chans), F32)
    conv, gated, local, mirrored, ahead, sub, sent = call(
        functools.partial(first_kernel, size),
        [stream] * 3
        + [
            ((chans, length + BLK), BF16),
            ((chans, BLK), BF16),
            blocks,
            ((n_ctx, modes, chans), F32),
        ],
        halo,
        q1,
        k1,
        v1,
        k2,
        short,
        long,
        close,
        rate_t,
        held=range(7),
        scratch=[pltpu.VMEM((chans, length), BF16)],
        name="first",
    )
    states = lax.all_to_all(sent, "ctx", 0, 0, tiled=True)
    conv2, gated2, *parts = call(
        functools.partial(second_kernel, size, groups),
        [stream] * 2 + [((width, length), BF16)] * n_ch,
        states,
        sub,
        rate_t,
        coef_t,
        reach,
        local,
        q2,
        weight,
        held=range(2),
        name="second",
    )
    mixed_parts = [parts[0]]
    for k in range(1, n_ch):
        mixed_parts.append(lax.ppermute(parts[k], "ch", around(n_ch, k)))
    if fused:
        sent_shape, spare = ((n_ctx, rows + modes // 2, out_chans), BF16), ((8, BLK), F32)
    else:
        sent_shape, spare = ((n_ctx, modes, chans), F32), ((chans, out_chans), F32)
    q2_grad, local_back, sub_back, edge, sent_back, weight_part = call(
        functools.partial(third_kernel, size, n_ch, fused),
        [stream] * 2 + [blocks, ((chans, 2 * BLK), BF16), sent_shape, spare],
        out_grad,
        *grads,
        weight,
        q2,
        conv2,
        gated2,
        long,
        open_,
        rate_t,
        coef_t,
        rate,
        ahead,
        scratch=[pltpu.VMEM((chans, length), BF16)],
        name="third",
    )
    states_back = lax.all_to_all(sent_back, "ctx", 0, 0, tiled=True)
    next_edge = lax.ppermute(edge, "ctx", around(n_ctx, -1))
    p2_grad, turned_grad, last = call(
        functools.partial(fourth_kernel, size, fused),
        [stream, ((chans, length + BLK), BF16), sent_shape if fused else ((groups, BLK), F32)],
        states_back,
        next_edge,
        sub_back,
        rate_t,
        coef_t,
        rate,
        local_back,
        late_q1,
        late_k2,
        mirrored,
        name="fourth",
    )
    scale = 1.0 / math.sqrt(length * n_ctx)
    if fused:
        final = lax.all_to_all(last, "ctx", 0, 0, tiled=True)
    else:
        weight_total, filter_total = lax.psum((weight_part, last), "ctx")
    q2_out, k2_out, q1_out, k1_out, v1_out = call(
        functools.partial(fifth_kernel, size),
        [stream] * 5,
        p2_grad,
        turned_grad,
        q2_grad,
        gated,
        conv,
        late_k2,
        late_k1,
        late_v1,
        short,
        name="fifth",
    )
    mixed = sum(p.astype(F32) for p in mixed_parts).astype(BF16)
    if fused:
        weight_grad, filter_grad = call(
            functools.partial(last_kernel, scale),
            [((n_ctx, rows, out_chans), F32), ((groups, BLK), F32)],
            final,
            name="last",
        )
        weight_grad = weight_grad.reshape(chans, out_chans)
    else:
        weight_grad = scale * weight_total
        filter_grad = scale * filter_total
    return (mixed, q1_out, k1_out, v1_out, q2_out, k2_out, weight_grad, filter_grad)


def solution(mesh):
    cut, rows_only = P("ch", "ctx"), P("ch", None)

    return jax.shard_map(
        on_device,
        mesh=mesh,
        in_specs=(cut,) * 6 + (rows_only,) * 4,
        out_specs=(cut,) * 6 + (rows_only,) * 2,
        check_vma=False,
    )
```

```python
import functools
import math

import jax
import jax.numpy as jnp
from jax import lax
from jax.experimental import pallas as pl
from jax.experimental.pallas import tpu as pltpu
from jax.sharding import PartitionSpec as P

BLK = 128
VMEM_LIMIT = 12 << 20
HIGHEST = lax.Precision.HIGHEST
F32 = jnp.float32
BF16 = jnp.bfloat16


def dot(a, b, ca=1, cb=0, precision=None):
    return lax.dot_general(
        a, b, (((ca,), (cb,)), ((), ())), preferred_element_type=F32, precision=precision
    )


def split(x):
    hi = x.astype(BF16)
    return hi, (x - hi.astype(F32)).astype(BF16)


def iota(shape, dim):
    return lax.broadcasted_iota(jnp.int32, shape, dim)


def rows_of(ref, g, size, first, count):
    return jnp.concatenate(
        [
            ref[g * size : (g + 1) * size, (first + b) * BLK : (first + b + 1) * BLK]
            for b in range(count)
        ],
        axis=0,
    )


def put_rows(ref, g, size, value):
    for b in range(value.shape[0] // size):
        ref[g * size : (g + 1) * size, b * BLK : (b + 1) * BLK] = value[
            b * size : (b + 1) * size
        ].astype(ref.dtype)


def circulant(row):
    return pltpu.roll(jnp.broadcast_to(row, (BLK, BLK)), 0, 1, stride=1, stride_axis=0)


def column(table):
    groups, modes = table.shape
    wide = jnp.broadcast_to(table[:, None, :], (groups, modes, modes)).reshape(-1, modes)
    diag = iota(wide.shape, 0) % modes == iota(wide.shape, 1)
    return jnp.sum(jnp.where(diag, wide, 0.0), axis=1, keepdims=True)


def meeting(rate, groups, modes):
    half = groups * modes
    hi, lo = split(jnp.exp(-column(rate) * (BLK - iota((half, BLK), 1).astype(F32))))
    return jnp.concatenate([hi, hi, lo], axis=0)


def per_channel(table, size):
    groups = table.shape[0]
    chans = groups * size
    pick = (iota((groups, chans), 1) // size == iota((groups, chans), 0)).astype(F32)
    return dot(table, pick, 0, 0, HIGHEST)


def block_states(table, stream, groups, modes, size):
    half = groups * modes
    chans = groups * size
    full = dot(table, stream, 1, 1)
    full = full[:half] + full[half:]
    own = iota((half, chans), 0) // modes == iota((half, chans), 1) // size
    return jnp.sum(jnp.where(own, full, 0.0).reshape(groups, modes, chans), axis=0)


def state_terms(states, table, groups, modes, size):
    chans = groups * size
    half = groups * modes
    count = len(states)
    hi, lo = split(jnp.concatenate(states, axis=1))
    pick = (iota((modes, half), 1) % modes == iota((modes, half), 0)).astype(BF16)
    own = (iota((count * chans, half), 0) % chans) // size == iota((count * chans, half), 1) // modes
    wide_hi = jnp.where(own, dot(hi, pick, 0, 0), 0.0).astype(BF16)
    wide_lo = jnp.where(own, dot(lo, pick, 0, 0), 0.0).astype(BF16)
    out = dot(jnp.concatenate([wide_hi, wide_lo, wide_hi], axis=1), table)
    return [out[i * chans : (i + 1) * chans] for i in range(count)]


def pack_rows(ref, first, value):
    half, chans = value.shape[0] // 2, value.shape[1]
    for i, part in enumerate(split(value)):
        for j in range(2):
            at = (2 * i + j) * chans
            ref[first:, at : at + chans] = part[j * half : (j + 1) * half]
    width = ref.shape[1]
    if 4 * chans < width:
        ref[first:, 4 * chans :] = jnp.zeros((half, width - 4 * chans), BF16)


def unpack_rows(ref, first, chans):
    parts = [ref[first:, i * chans : (i + 1) * chans].astype(F32) for i in range(4)]
    return jnp.concatenate([parts[0] + parts[2], parts[1] + parts[3]], axis=0)


def tables_kernel(size, held, *refs):
    taps, rate, coef = refs[:3]
    sources = refs[3 : 3 + held]
    (short, long, close, open_, reach, rate_t, coef_t) = refs[3 + held : 10 + held]
    targets, sems = refs[10 + held : -1], refs[-1]
    copies = [
        pltpu.make_async_copy(source, target, sems.at[i])
        for i, (source, target) in enumerate(zip(sources, targets))
    ]
    for copy in copies:
        copy.start()
    groups, modes = rate.shape
    half = groups * modes
    col, coef_col = column(rate[...]), column(coef[...])
    at = iota((half, BLK), 1).astype(F32)
    falling = jnp.exp(-col * at)
    hi, lo = split(falling)
    open_[0:half] = hi
    open_[half:] = lo
    hi, lo = split(jnp.exp(-col * (BLK - 1.0 - at)))
    close[0:half] = hi
    close[half:] = lo
    hi, lo = split(jnp.exp(-col * (at + 1.0)))
    reach[0:half] = hi
    reach[half : 2 * half] = hi
    reach[2 * half :] = lo
    kernel = jnp.sum((coef_col * falling).reshape(groups, modes, BLK), axis=1)
    tap_rows = taps[...].astype(F32)
    later = iota((BLK, BLK), 1) >= iota((BLK, BLK), 0)
    for g in range(groups):
        turned = circulant(tap_rows[g : g + 1])
        short[g, 0:BLK] = jnp.where(later, 0.0, turned).astype(BF16)
        short[g, BLK:] = jnp.where(later, turned, 0.0).astype(BF16)
        long[g] = jnp.where(later, circulant(kernel[g : g + 1]), 0.0).astype(BF16)
    rate_t[...] = per_channel(rate[...], size)
    coef_t[...] = per_channel(coef[...], size)
    for copy in copies:
        copy.wait()


def first_kernel(
    size,
    halo,
    q1,
    k1,
    v1,
    k2,
    short,
    long,
    close,
    rate_t,
    conv,
    gated,
    local,
    mirrored,
    ahead,
    sub,
    sent,
    stream,
):
    groups = short.shape[0]
    modes = rate_t.shape[0]
    count = q1.shape[1] // BLK
    seen = jnp.where(lax.axis_index("ctx") > 0, halo[...], jnp.zeros(halo.shape, BF16))
    mirror = (iota((BLK, BLK), 1) + iota((BLK, BLK), 0) == BLK - 1).astype(BF16)
    for g in range(groups):
        rows = slice(g * size, (g + 1) * size)
        p1 = (rows_of(k1, g, size, 0, count).astype(F32) * rows_of(v1, g, size, 0, count).astype(F32)).astype(BF16)
        before = jnp.concatenate([seen[rows], p1[: (count - 1) * size]], axis=0)
        c1 = dot(jnp.concatenate([before, p1], axis=1), short[g])
        put_rows(conv, g, size, c1)
        g1 = (rows_of(q1, g, size, 0, count).astype(F32) * c1).astype(BF16)
        put_rows(gated, g, size, g1)
        p2 = (rows_of(k2, g, size, 0, count).astype(F32) * g1.astype(F32)).astype(BF16)
        put_rows(stream, g, size, p2)
        put_rows(local, g, size, dot(p2, long[g]))
    mirrored[:, :BLK] = dot(seen, mirror).astype(BF16)
    ahead[...] = (k2[:, :BLK].astype(F32) * q1[:, :BLK].astype(F32)).astype(BF16)
    for b in range(count):
        cols = slice(b * BLK, (b + 1) * BLK)
        p1 = (k1[:, cols].astype(F32) * v1[:, cols].astype(F32)).astype(BF16)
        mirrored[:, (b + 1) * BLK : (b + 2) * BLK] = dot(p1, mirror).astype(BF16)
    decay = jnp.exp(-rate_t[...] * BLK)
    total = None
    for b in range(count):
        state = block_states(close[...], stream[:, b * BLK : (b + 1) * BLK], groups, modes, size)
        sub[b] = state
        total = state if total is None else total * decay + state
    for d in range(sent.shape[0]):
        sent[d] = total


def second_kernel(
    size, groups, states, sub, rate_t, coef_t, reach, local, q2, weight, conv2, gated2, *parts
):
    modes = rate_t.shape[0]
    ctx_size, count = states.shape[0], sub.shape[0]
    length = float(count * BLK)
    me = lax.axis_index("ctx")
    rate = rate_t[...]
    entering = jnp.zeros(rate.shape, F32)
    for d in range(ctx_size):
        gap = me - 1 - d
        factor = jnp.exp(-rate * (length * jnp.maximum(gap, 0).astype(F32)))
        entering = entering + jnp.where(gap >= 0, factor * states[d], 0.0)
    decay = jnp.exp(-rate * BLK)
    coefs = coef_t[...]
    all_states = []
    for b in range(count):
        all_states.append(coefs * entering)
        entering = decay * entering + sub[b]
    terms = state_terms(all_states, reach[...], groups, modes, size)
    for b in range(count):
        cols = slice(b * BLK, (b + 1) * BLK)
        c2 = (local[:, cols].astype(F32) + terms[b]).astype(BF16)
        conv2[:, cols] = c2
        gated2[:, cols] = (q2[:, cols].astype(F32) * c2.astype(F32)).astype(BF16)
    here = lax.axis_index("ch")
    width = weight.shape[1] // len(parts)
    for k, part in enumerate(parts):
        at = pl.multiple_of(lax.rem(here + k, len(parts)) * width, BLK)
        part[...] = dot(weight[:, pl.ds(at, width)], gated2[...], 0, 0).astype(BF16)


def third_kernel(size, n_ch, n_ctx, fused, *refs):
    grads = refs[:n_ch]
    (weight, q2, conv2, gated2, long, open_, rate_t) = refs[n_ch : n_ch + 7]
    (q2_grad, local, sub, first, *sent) = refs[n_ch + 7 : -2]
    whole, stream = refs[-2:]
    groups = long.shape[0]
    modes, chans = rate_t.shape
    count = q2.shape[1] // BLK
    here = lax.axis_index("ch")
    width = weight.shape[1] // n_ch
    starts = [
        pl.multiple_of(lax.rem(here - k + n_ch, n_ch) * width, BLK) for k in range(n_ch)
    ]
    acc = None
    for k in range(n_ch):
        term = dot(weight[:, pl.ds(starts[k], width)], grads[k][...])
        acc = term if acc is None else acc + term
    q2_grad[...] = (acc * conv2[...].astype(F32)).astype(BF16)
    stream[...] = (acc * q2[...].astype(F32)).astype(BF16)
    for g in range(groups):
        put_rows(local, g, size, dot(rows_of(stream, g, size, 0, count), long[g], 1, 1))
    decay = jnp.exp(-rate_t[...] * BLK)
    total = None
    for b in reversed(range(count)):
        state = block_states(open_[...], stream[:, b * BLK : (b + 1) * BLK], groups, modes, size)
        sub[b] = state
        total = state if total is None else total * decay + state
    first[...] = local[:, :BLK]
    for k in range(n_ch):
        part = dot(gated2[...], grads[k][...], 1, 1)
        if fused:
            whole[:, pl.ds(starts[k], width)] = part.astype(BF16)
        else:
            sent[1][:, pl.ds(starts[k], width)] = part
    if fused:
        rows = chans // n_ctx
        me = lax.axis_index("ctx")
        for k in range(n_ctx):
            at = pl.multiple_of(jnp.bitwise_xor(me, k) * rows, rows)
            sent[k][0:rows] = whole[pl.ds(at, rows), :]
            pack_rows(sent[k], rows, total)
    else:
        for d in range(n_ctx):
            sent[0][d] = total


def between_kernel(size, local, sub, rate_t, coef_t, rate_g, ahead, edge):
    modes, chans = rate_t.shape
    count = sub.shape[0]
    decay = jnp.exp(-rate_t[...] * BLK)
    inner = sub[count - 1]
    for b in reversed(range(1, count - 1)):
        inner = inner * decay + sub[b]
    meet = meeting(rate_g[...], chans // size, modes)
    (term,) = state_terms([coef_t[...] * inner], meet, chans // size, modes, size)
    edge[:, :BLK] = (local[...].astype(F32) + term).astype(BF16)
    edge[:, BLK:] = ahead[...]


def fourth_kernel(size, fused, n_ctx, *refs):
    moved = refs[: n_ctx if fused else 1]
    (sub, rate_t, coef_t, rate_g, local, q1, k2, mirrored) = refs[len(moved) : len(moved) + 8]
    (beside, p2_grad, turned_grad, out) = refs[len(moved) + 8 :]
    modes, chans = rate_t.shape
    groups = chans // size
    count = sub.shape[0]
    length = float(count * BLK)
    rows = chans // n_ctx
    me = lax.axis_index("ctx")
    rate = rate_t[...]
    coefs = coef_t[...]
    beyond = jnp.zeros(rate.shape, F32)
    following = jnp.zeros(rate.shape, F32)
    for k in range(n_ctx):
        state = unpack_rows(moved[k], rows, chans) if fused else moved[0][k]
        gap = (jnp.bitwise_xor(me, k) if fused else k) - me - 2
        factor = jnp.exp(-rate * (length * jnp.maximum(gap, 0).astype(F32)))
        beyond = beyond + jnp.where(gap >= 0, factor * state, 0.0)
        following = following + jnp.where(gap == -1, state, 0.0)
    decay = jnp.exp(-rate * BLK)
    entering = jnp.exp(-rate * length) * beyond + following
    all_states = [coefs * (jnp.exp(-rate * (length - BLK)) * beyond)]
    for b in reversed(range(count)):
        all_states.append(coefs * entering)
        entering = decay * entering + sub[b]
    terms = state_terms(all_states, meeting(rate_g[...], groups, modes), groups, modes, size)
    beside[...] = terms[0]
    for b in range(count):
        cols = slice(b * BLK, (b + 1) * BLK)
        p2g = (local[:, cols].astype(F32) + terms[count - b]).astype(BF16)
        p2_grad[:, cols] = p2g
        g1g = p2g.astype(F32) * k2[:, cols].astype(F32)
        turned_grad[:, cols] = (g1g * q1[:, cols].astype(F32)).astype(BF16)
    later = iota((BLK, BLK), 1) + iota((BLK, BLK), 0) >= BLK - 1
    filters = []
    for g in range(groups):
        here = rows_of(turned_grad, g, size, 0, count)
        seen = rows_of(mirrored, g, size, 0, count + 1)
        inside = dot(seen[size:], here, 0, 0)
        across = dot(seen[: count * size], here, 0, 0)
        turned = pltpu.roll(jnp.where(later, inside, across), 1, 1, stride=1, stride_axis=0)
        filters.append(jnp.sum(turned, axis=0, keepdims=True))
    filter_rows = jnp.concatenate(filters, axis=0)
    if fused:
        total = moved[0][0:rows].astype(F32)
        for k in range(1, n_ctx):
            total = total + moved[k][0:rows].astype(F32)
        out[0:rows] = total.astype(BF16)
        pack_rows(out, rows, filter_rows)
    else:
        out[...] = filter_rows


def fifth_kernel(size, ctx_size, p2_grad, turned_grad, beside, edge, q2_grad, gated, conv, k2, k1, v1, short, q2_out, k2_out, q1_out, k1_out, v1_out, next_grad):
    groups = short.shape[0]
    count = p2_grad.shape[1] // BLK
    q2_out[...] = q2_grad[...]
    p2g = p2_grad[...].astype(F32)
    k2_out[...] = (p2g * gated[...].astype(F32)).astype(BF16)
    q1_out[...] = (p2g * k2[...].astype(F32) * conv[...].astype(F32)).astype(BF16)
    next_p = (edge[:, :BLK].astype(F32) + beside[...]).astype(BF16)
    near = (next_p.astype(F32) * edge[:, BLK:].astype(F32)).astype(BF16)
    last = lax.axis_index("ctx") == ctx_size - 1
    next_grad[...] = jnp.where(last, jnp.zeros(near.shape, BF16), near)
    for g in range(groups):
        kv, vv = rows_of(k1, g, size, 0, count).astype(F32), rows_of(v1, g, size, 0, count).astype(F32)
        here = rows_of(turned_grad, g, size, 0, count)
        after = jnp.concatenate([here[size:], next_grad[g * size : (g + 1) * size]], axis=0)
        p1g = dot(here, short[g, BLK:], 1, 1) + dot(after, short[g, 0:BLK], 1, 1)
        put_rows(k1_out, g, size, p1g * vv)
        put_rows(v1_out, g, size, p1g * kv)


def last_kernel(scale, n_ctx, *refs):
    moved, parts, (weight_out, filter_out, mixed) = refs[:n_ctx], refs[n_ctx:-3], refs[-3:]
    rows = weight_out.shape[1]
    me = lax.axis_index("ctx")
    total = None
    for k in range(n_ctx):
        weight_out[jnp.bitwise_xor(me, k)] = scale * moved[k][0:rows].astype(F32)
        term = unpack_rows(moved[k], rows, BLK)
        total = term if total is None else total + term
    filter_out[...] = scale * total
    summed = parts[0][...].astype(F32)
    for part in parts[1:]:
        summed = summed + part[...].astype(F32)
    mixed[...] = summed.astype(BF16)


def call(kernel, outs, *args, held=(), far=(), scratch=(), name):
    size = sum(math.prod(a.shape) * a.dtype.itemsize for a in args)
    size += sum(math.prod(s) * jnp.dtype(t).itemsize for s, t in outs)
    args = [pltpu.with_memory_space_constraint(a, pltpu.HBM) if i in far else a for i, a in enumerate(args)]
    results = pl.pallas_call(
        kernel,
        out_shape=[
            pltpu.VMEM(s, t) if i in held else pltpu.HBM(s, t) for i, (s, t) in enumerate(outs)
        ],
        in_specs=[
            pl.BlockSpec(memory_space=pltpu.HBM if name == "tables" and i > 2 else pltpu.VMEM)
            for i in range(len(args))
        ],
        out_specs=[pl.BlockSpec(memory_space=pltpu.VMEM)] * len(outs),
        scratch_shapes=list(scratch),
        cost_estimate=pl.CostEstimate(flops=0, bytes_accessed=size, transcendentals=0),
        compiler_params=pltpu.CompilerParams(vmem_limit_bytes=VMEM_LIMIT),
    )(*args)
    return [
        pltpu.with_memory_space_constraint(o, pltpu.VMEM) if i in held else o
        for i, o in enumerate(results)
    ]


def around(count, step):
    return [(i, (i + step) % count) for i in range(count)]


def exchange(blocks, count):
    out = [blocks[0]]
    for k in range(1, count):
        out.append(lax.ppermute(blocks[k], "ctx", [(i, i ^ k) for i in range(count)]))
    return out


def gather(block, count):
    out = {0: block}
    for k in [1] + list(range(2, count, 2)):
        out[k] = lax.ppermute(block, "ctx", [(i, i ^ k) for i in range(count)])
    for k in range(2, count, 2):
        out[k + 1] = lax.ppermute(out[k], "ctx", [(i, i ^ 1) for i in range(count)])
    return [out[k] for k in range(count)]


def on_device(q1, k1, v1, q2, k2, out_grad, taps, rate, residue, weight):
    chans, length = q1.shape
    groups, _ = taps.shape
    modes = rate.shape[1]
    size = chans // groups
    half = groups * modes
    count = length // BLK
    n_ctx, n_ch = lax.axis_size("ctx"), lax.axis_size("ch")
    rows = chans // n_ctx
    fused = rows % 16 == 0 and groups == modes == 16 and 4 * chans == weight.shape[1]
    fused = fused and n_ctx & (n_ctx - 1) == 0
    out_chans = weight.shape[1]
    width = out_chans // n_ch

    tail = (k1[:, length - BLK :].astype(F32) * v1[:, length - BLK :].astype(F32)).astype(BF16)
    halo = lax.ppermute(tail, "ctx", around(n_ctx, 1))
    grads = []
    for k in range(1, n_ch):
        grads.append(lax.ppermute(out_grad, "ch", around(n_ch, k)))

    coef = residue * jnp.sqrt(-jnp.expm1(-2.0 * rate))
    loaded = [
        pltpu.with_memory_space_constraint(a, pltpu.HBM)
        for a in (q1, k1, v1, q2, k2, out_grad, weight)
    ]
    late_q1, late_k1, late_v1, _, late_k2 = loaded[:5]
    short, long, close, open_, reach, rate_t, coef_t, q1, k1, v1, q2, k2, out_grad, weight = call(
        functools.partial(tables_kernel, size, len(loaded)),
        [
            ((groups, 2 * BLK, BLK), BF16),
            ((groups, BLK, BLK), BF16),
            ((2 * half, BLK), BF16),
            ((2 * half, BLK), BF16),
            ((3 * half, BLK), BF16),
            ((modes, chans), F32),
            ((modes, chans), F32),
        ]
        + [(a.shape, a.dtype) for a in loaded],
        taps,
        rate,
        coef,
        *loaded,
        held=range(14),
        scratch=[pltpu.SemaphoreType.DMA((len(loaded),))],
        name="tables",
    )
    stream = ((chans, length), BF16)
    blocks = ((count, modes, chans), F32)
    conv, gated, local, mirrored, ahead, sub, sent = call(
        functools.partial(first_kernel, size),
        [stream] * 3
        + [
            ((chans, length + BLK), BF16),
            ((chans, BLK), BF16),
            blocks,
            ((n_ctx, modes, chans), F32),
        ],
        halo,
        q1,
        k1,
        v1,
        k2,
        short,
        long,
        close,
        rate_t,
        held=(2, 3, 5, 6),
        scratch=[pltpu.VMEM((chans, length), BF16)],
        name="first",
    )
    states = lax.all_to_all(sent, "ctx", 0, 0, tiled=True)
    conv2, gated2, *parts = call(
        functools.partial(second_kernel, size, groups),
        [stream] * 2 + [((width, length), BF16)] * n_ch,
        states,
        sub,
        rate_t,
        coef_t,
        reach,
        local,
        q2,
        weight,
        held=range(2),
        name="second",
    )
    mixed_parts = [parts[0]]
    for k in range(1, n_ch):
        mixed_parts.append(lax.ppermute(parts[k], "ch", around(n_ch, k)))
    packed = ((rows + modes // 2, out_chans), BF16)
    if fused:
        sent_shapes = [packed] * n_ctx
    else:
        sent_shapes = [((n_ctx, modes, chans), F32), ((chans, out_chans), F32)]
    q2_grad, local_back, sub_back, first_back, *sent_back = call(
        functools.partial(third_kernel, size, n_ch, n_ctx, fused),
        [stream] * 2 + [blocks, ((chans, BLK), BF16)] + sent_shapes,
        out_grad,
        *grads,
        weight,
        q2,
        conv2,
        gated2,
        long,
        open_,
        rate_t,
        scratch=[pltpu.VMEM((chans, out_chans), BF16), pltpu.VMEM((chans, length), BF16)],
        name="third",
    )
    if fused:
        states_back = exchange(sent_back, n_ctx)
    else:
        states_back = [lax.all_to_all(sent_back[0], "ctx", 0, 0, tiled=True)]
    (edge,) = call(
        functools.partial(between_kernel, size),
        [((chans, 2 * BLK), BF16)],
        first_back,
        sub_back,
        rate_t,
        coef_t,
        rate,
        ahead,
        far=(0, 1, 5),
        name="between",
    )
    next_edge = lax.ppermute(edge, "ctx", around(n_ctx, -1))
    beside, p2_grad, turned_grad, last = call(
        functools.partial(fourth_kernel, size, fused, n_ctx),
        [((chans, BLK), F32), stream, stream, packed if fused else ((groups, BLK), F32)],
        *states_back,
        sub_back,
        rate_t,
        coef_t,
        rate,
        local_back,
        late_q1,
        late_k2,
        mirrored,
        far=(0, n_ctx) if fused else (),
        name="fourth",
    )
    scale = 1.0 / math.sqrt(length * n_ctx)
    if fused:
        final = gather(last, n_ctx)
    else:
        weight_total, filter_total = lax.psum((sent_back[1], last), "ctx")
    q2_out, k2_out, q1_out, k1_out, v1_out = call(
        functools.partial(fifth_kernel, size, n_ctx),
        [stream] * 5,
        p2_grad,
        turned_grad,
        beside,
        next_edge,
        q2_grad,
        gated,
        conv,
        late_k2,
        late_k1,
        late_v1,
        short,
        far=(0, 1, 2, 4, 5, 6),
        scratch=[pltpu.VMEM((chans, BLK), BF16)],
        name="fifth",
    )
    if fused:
        weight_grad, filter_grad, mixed = call(
            functools.partial(last_kernel, scale, n_ctx),
            [((n_ctx, rows, out_chans), F32), ((groups, BLK), F32), ((width, length), BF16)],
            *final,
            *mixed_parts,
            name="last",
        )
        weight_grad = weight_grad.reshape(chans, out_chans)
    else:
        weight_grad = scale * weight_total
        mixed = sum(p.astype(F32) for p in mixed_parts).astype(BF16)
        filter_grad = scale * filter_total
    return (mixed, q1_out, k1_out, v1_out, q2_out, k2_out, weight_grad, filter_grad)


def solution(mesh):
    cut, rows_only = P("ch", "ctx"), P("ch", None)

    return jax.shard_map(
        on_device,
        mesh=mesh,
        in_specs=(cut,) * 6 + (rows_only,) * 4,
        out_specs=(cut,) * 6 + (rows_only,) * 2,
        check_vma=False,
    )
```

```python
import functools
import math

import jax
import jax.numpy as jnp
from jax import lax
from jax.experimental import pallas as pl
from jax.experimental.pallas import tpu as pltpu
from jax.sharding import PartitionSpec as P

BLK = 128
VMEM_LIMIT = 12 << 20
HIGHEST = lax.Precision.HIGHEST
F32 = jnp.float32
BF16 = jnp.bfloat16


def dot(a, b, ca=1, cb=0, precision=None):
    return lax.dot_general(
        a, b, (((ca,), (cb,)), ((), ())), preferred_element_type=F32, precision=precision
    )


def split(x):
    hi = x.astype(BF16)
    return hi, (x - hi.astype(F32)).astype(BF16)


def iota(shape, dim):
    return lax.broadcasted_iota(jnp.int32, shape, dim)


def rows_of(ref, g, size, first, count):
    return jnp.concatenate(
        [
            ref[g * size : (g + 1) * size, (first + b) * BLK : (first + b + 1) * BLK]
            for b in range(count)
        ],
        axis=0,
    )


def put_rows(ref, g, size, value):
    for b in range(value.shape[0] // size):
        ref[g * size : (g + 1) * size, b * BLK : (b + 1) * BLK] = value[
            b * size : (b + 1) * size
        ].astype(ref.dtype)


def circulant(row):
    return pltpu.roll(jnp.broadcast_to(row, (BLK, BLK)), 0, 1, stride=1, stride_axis=0)


def column(table):
    groups, modes = table.shape
    wide = jnp.broadcast_to(table[:, None, :], (groups, modes, modes)).reshape(-1, modes)
    diag = iota(wide.shape, 0) % modes == iota(wide.shape, 1)
    return jnp.sum(jnp.where(diag, wide, 0.0), axis=1, keepdims=True)


def meeting(rate, groups, modes):
    half = groups * modes
    hi, lo = split(jnp.exp(-column(rate) * (BLK - iota((half, BLK), 1).astype(F32))))
    return jnp.concatenate([hi, hi, lo], axis=0)


def per_channel(table, size):
    groups = table.shape[0]
    chans = groups * size
    pick = (iota((groups, chans), 1) // size == iota((groups, chans), 0)).astype(F32)
    return dot(table, pick, 0, 0, HIGHEST)


def block_states(table, stream, groups, modes, size):
    half = groups * modes
    chans = groups * size
    full = dot(table, stream, 1, 1)
    full = full[:half] + full[half:]
    own = iota((half, chans), 0) // modes == iota((half, chans), 1) // size
    return jnp.sum(jnp.where(own, full, 0.0).reshape(groups, modes, chans), axis=0)


def state_terms(states, table, groups, modes, size):
    chans = groups * size
    half = groups * modes
    count = len(states)
    hi, lo = split(jnp.concatenate(states, axis=1))
    pick = (iota((modes, half), 1) % modes == iota((modes, half), 0)).astype(BF16)
    own = (iota((count * chans, half), 0) % chans) // size == iota((count * chans, half), 1) // modes
    wide_hi = jnp.where(own, dot(hi, pick, 0, 0), 0.0).astype(BF16)
    wide_lo = jnp.where(own, dot(lo, pick, 0, 0), 0.0).astype(BF16)
    out = dot(jnp.concatenate([wide_hi, wide_lo, wide_hi], axis=1), table)
    return [out[i * chans : (i + 1) * chans] for i in range(count)]


def pack_rows(ref, first, value):
    half, chans = value.shape[0] // 2, value.shape[1]
    for i, part in enumerate(split(value)):
        for j in range(2):
            at = (2 * i + j) * chans
            ref[first : first + half, at : at + chans] = part[j * half : (j + 1) * half]
    width = ref.shape[1]
    if 4 * chans < width:
        ref[first : first + half, 4 * chans :] = jnp.zeros((half, width - 4 * chans), BF16)


def unpack_rows(ref, first, half, chans):
    parts = [ref[first : first + half, i * chans : (i + 1) * chans].astype(F32) for i in range(4)]
    return jnp.concatenate([parts[0] + parts[2], parts[1] + parts[3]], axis=0)


def tables_kernel(size, held, *refs):
    taps, rate, coef = refs[:3]
    sources = refs[3 : 3 + held]
    (short, long, close, open_, reach, rate_t, coef_t) = refs[3 + held : 10 + held]
    targets, sems = refs[10 + held : -1], refs[-1]
    copies = [
        pltpu.make_async_copy(source, target, sems.at[i])
        for i, (source, target) in enumerate(zip(sources, targets))
    ]
    for copy in copies:
        copy.start()
    groups, modes = rate.shape
    half = groups * modes
    col, coef_col = column(rate[...]), column(coef[...])
    at = iota((half, BLK), 1).astype(F32)
    falling = jnp.exp(-col * at)
    hi, lo = split(falling)
    open_[0:half] = hi
    open_[half:] = lo
    hi, lo = split(jnp.exp(-col * (BLK - 1.0 - at)))
    close[0:half] = hi
    close[half:] = lo
    hi, lo = split(jnp.exp(-col * (at + 1.0)))
    reach[0:half] = hi
    reach[half : 2 * half] = hi
    reach[2 * half :] = lo
    kernel = jnp.sum((coef_col * falling).reshape(groups, modes, BLK), axis=1)
    tap_rows = taps[...].astype(F32)
    later = iota((BLK, BLK), 1) >= iota((BLK, BLK), 0)
    for g in range(groups):
        turned = circulant(tap_rows[g : g + 1])
        short[g, 0:BLK] = jnp.where(later, 0.0, turned).astype(BF16)
        short[g, BLK:] = jnp.where(later, turned, 0.0).astype(BF16)
        long[g] = jnp.where(later, circulant(kernel[g : g + 1]), 0.0).astype(BF16)
    rate_t[...] = per_channel(rate[...], size)
    coef_t[...] = per_channel(coef[...], size)
    for copy in copies:
        copy.wait()


def first_kernel(
    size,
    halo,
    q1,
    k1,
    v1,
    k2,
    short,
    long,
    close,
    rate_t,
    conv,
    gated,
    local,
    mirrored,
    ahead,
    sub,
    sent,
    stream,
):
    groups = short.shape[0]
    modes = rate_t.shape[0]
    count = q1.shape[1] // BLK
    seen = jnp.where(lax.axis_index("ctx") > 0, halo[...], jnp.zeros(halo.shape, BF16))
    mirror = (iota((BLK, BLK), 1) + iota((BLK, BLK), 0) == BLK - 1).astype(BF16)
    for g in range(groups):
        rows = slice(g * size, (g + 1) * size)
        p1 = (rows_of(k1, g, size, 0, count).astype(F32) * rows_of(v1, g, size, 0, count).astype(F32)).astype(BF16)
        before = jnp.concatenate([seen[rows], p1[: (count - 1) * size]], axis=0)
        c1 = dot(jnp.concatenate([before, p1], axis=1), short[g])
        put_rows(conv, g, size, c1)
        g1 = (rows_of(q1, g, size, 0, count).astype(F32) * c1).astype(BF16)
        put_rows(gated, g, size, g1)
        p2 = (rows_of(k2, g, size, 0, count).astype(F32) * g1.astype(F32)).astype(BF16)
        put_rows(stream, g, size, p2)
        put_rows(local, g, size, dot(p2, long[g]))
    mirrored[:, :BLK] = dot(seen, mirror).astype(BF16)
    ahead[...] = (k2[:, :BLK].astype(F32) * q1[:, :BLK].astype(F32)).astype(BF16)
    for b in range(count):
        cols = slice(b * BLK, (b + 1) * BLK)
        p1 = (k1[:, cols].astype(F32) * v1[:, cols].astype(F32)).astype(BF16)
        mirrored[:, (b + 1) * BLK : (b + 2) * BLK] = dot(p1, mirror).astype(BF16)
    decay = jnp.exp(-rate_t[...] * BLK)
    total = None
    for b in range(count):
        state = block_states(close[...], stream[:, b * BLK : (b + 1) * BLK], groups, modes, size)
        sub[b] = state
        total = state if total is None else total * decay + state
    for d in range(sent.shape[0]):
        sent[d] = total


def second_kernel(
    size, groups, states, sub, rate_t, coef_t, reach, local, q2, weight, conv2, gated2, *parts
):
    modes = rate_t.shape[0]
    ctx_size, count = states.shape[0], sub.shape[0]
    length = float(count * BLK)
    me = lax.axis_index("ctx")
    rate = rate_t[...]
    entering = jnp.zeros(rate.shape, F32)
    for d in range(ctx_size):
        gap = me - 1 - d
        factor = jnp.exp(-rate * (length * jnp.maximum(gap, 0).astype(F32)))
        entering = entering + jnp.where(gap >= 0, factor * states[d], 0.0)
    decay = jnp.exp(-rate * BLK)
    coefs = coef_t[...]
    all_states = []
    for b in range(count):
        all_states.append(coefs * entering)
        entering = decay * entering + sub[b]
    terms = state_terms(all_states, reach[...], groups, modes, size)
    for b in range(count):
        cols = slice(b * BLK, (b + 1) * BLK)
        c2 = (local[:, cols].astype(F32) + terms[b]).astype(BF16)
        conv2[:, cols] = c2
        gated2[:, cols] = (q2[:, cols].astype(F32) * c2.astype(F32)).astype(BF16)
    here = lax.axis_index("ch")
    width = weight.shape[1] // len(parts)
    for k, part in enumerate(parts):
        at = pl.multiple_of(lax.rem(here + k, len(parts)) * width, BLK)
        part[...] = dot(weight[:, pl.ds(at, width)], gated2[...], 0, 0).astype(BF16)


def third_kernel(size, n_ch, n_ctx, fused, *refs):
    grads = refs[:n_ch]
    (weight, q2, conv2, gated2, long, open_, rate_t) = refs[n_ch : n_ch + 7]
    (q2_grad, local, sub, first, *sent) = refs[n_ch + 7 : -2]
    whole, stream = refs[-2:]
    groups = long.shape[0]
    modes, chans = rate_t.shape
    count = q2.shape[1] // BLK
    here = lax.axis_index("ch")
    width = weight.shape[1] // n_ch
    starts = [
        pl.multiple_of(lax.rem(here - k + n_ch, n_ch) * width, BLK) for k in range(n_ch)
    ]
    acc = None
    for k in range(n_ch):
        term = dot(weight[:, pl.ds(starts[k], width)], grads[k][...])
        acc = term if acc is None else acc + term
    q2_grad[...] = (acc * conv2[...].astype(F32)).astype(BF16)
    stream[...] = (acc * q2[...].astype(F32)).astype(BF16)
    for g in range(groups):
        put_rows(local, g, size, dot(rows_of(stream, g, size, 0, count), long[g], 1, 1))
    decay = jnp.exp(-rate_t[...] * BLK)
    total = None
    for b in reversed(range(count)):
        state = block_states(open_[...], stream[:, b * BLK : (b + 1) * BLK], groups, modes, size)
        sub[b] = state
        total = state if total is None else total * decay + state
    first[...] = local[:, :BLK]
    for k in range(n_ch):
        part = dot(gated2[...], grads[k][...], 1, 1)
        if fused:
            whole[:, pl.ds(starts[k], width)] = part.astype(BF16)
        else:
            sent[1][:, pl.ds(starts[k], width)] = part
    if fused:
        rows = chans // n_ctx
        me = lax.axis_index("ctx")
        for i in range(n_ctx // 2):
            for j in range(2):
                at = pl.multiple_of(jnp.bitwise_xor(me, 2 * i + j) * rows, rows)
                sent[j][i * rows : (i + 1) * rows] = whole[pl.ds(at, rows), :]
        pack_rows(sent[1], n_ctx // 2 * rows, total)
        pack_rows(sent[2], 0, total)
    else:
        for d in range(n_ctx):
            sent[0][d] = total


def pair_kernel(size, kept, own, got, local, sub, rate_t, coef_t, rate_g, ahead, edge, *out):
    half = own.shape[0]
    rows = kept.shape[0] // len(out)
    for i, block in enumerate(out):
        at = slice(i * rows, (i + 1) * rows)
        block[0:rows] = (kept[at].astype(F32) + got[at].astype(F32)).astype(BF16)
        block[rows : rows + half] = own[...]
        block[rows + half :] = got[len(out) * rows :]
    between_kernel(size, local, sub, rate_t, coef_t, rate_g, ahead, edge)


def between_kernel(size, local, sub, rate_t, coef_t, rate_g, ahead, edge):
    modes, chans = rate_t.shape
    count = sub.shape[0]
    decay = jnp.exp(-rate_t[...] * BLK)
    inner = sub[count - 1]
    for b in reversed(range(1, count - 1)):
        inner = inner * decay + sub[b]
    meet = meeting(rate_g[...], chans // size, modes)
    (term,) = state_terms([coef_t[...] * inner], meet, chans // size, modes, size)
    edge[:, :BLK] = (local[...].astype(F32) + term).astype(BF16)
    edge[:, BLK:] = ahead[...]


def fourth_kernel(size, fused, n_ctx, *refs):
    moved = refs[: n_ctx // 2 if fused else 1]
    (sub, rate_t, coef_t, rate_g, local, q1, k2, mirrored) = refs[len(moved) : len(moved) + 8]
    (beside, p2_grad, turned_grad, out) = refs[len(moved) + 8 :]
    modes, chans = rate_t.shape
    groups = chans // size
    count = sub.shape[0]
    length = float(count * BLK)
    rows = chans // n_ctx
    me = lax.axis_index("ctx")
    rate = rate_t[...]
    coefs = coef_t[...]
    beyond = jnp.zeros(rate.shape, F32)
    following = jnp.zeros(rate.shape, F32)
    for k in range(n_ctx):
        if fused:
            at = rows + k % 2 * (modes // 2)
            state = unpack_rows(moved[k // 2], at, modes // 2, chans)
        else:
            state = moved[0][k]
        gap = (jnp.bitwise_xor(me, k) if fused else k) - me - 2
        factor = jnp.exp(-rate * (length * jnp.maximum(gap, 0).astype(F32)))
        beyond = beyond + jnp.where(gap >= 0, factor * state, 0.0)
        following = following + jnp.where(gap == -1, state, 0.0)
    decay = jnp.exp(-rate * BLK)
    entering = jnp.exp(-rate * length) * beyond + following
    all_states = [coefs * (jnp.exp(-rate * (length - BLK)) * beyond)]
    for b in reversed(range(count)):
        all_states.append(coefs * entering)
        entering = decay * entering + sub[b]
    terms = state_terms(all_states, meeting(rate_g[...], groups, modes), groups, modes, size)
    beside[...] = terms[0]
    for b in range(count):
        cols = slice(b * BLK, (b + 1) * BLK)
        p2g = (local[:, cols].astype(F32) + terms[count - b]).astype(BF16)
        p2_grad[:, cols] = p2g
        g1g = p2g.astype(F32) * k2[:, cols].astype(F32)
        turned_grad[:, cols] = (g1g * q1[:, cols].astype(F32)).astype(BF16)
    later = iota((BLK, BLK), 1) + iota((BLK, BLK), 0) >= BLK - 1
    filters = []
    for g in range(groups):
        here = rows_of(turned_grad, g, size, 0, count)
        seen = rows_of(mirrored, g, size, 0, count + 1)
        inside = dot(seen[size:], here, 0, 0)
        across = dot(seen[: count * size], here, 0, 0)
        turned = pltpu.roll(jnp.where(later, inside, across), 1, 1, stride=1, stride_axis=0)
        filters.append(jnp.sum(turned, axis=0, keepdims=True))
    filter_rows = jnp.concatenate(filters, axis=0)
    if fused:
        total = moved[0][0:rows].astype(F32)
        for block in moved[1:]:
            total = total + block[0:rows].astype(F32)
        out[0:rows] = total.astype(BF16)
        pack_rows(out, rows, filter_rows)
    else:
        out[...] = filter_rows


def fifth_kernel(size, ctx_size, p2_grad, turned_grad, beside, edge, q2_grad, gated, conv, k2, k1, v1, short, q2_out, k2_out, q1_out, k1_out, v1_out, next_grad):
    groups = short.shape[0]
    count = p2_grad.shape[1] // BLK
    q2_out[...] = q2_grad[...]
    p2g = p2_grad[...].astype(F32)
    k2_out[...] = (p2g * gated[...].astype(F32)).astype(BF16)
    q1_out[...] = (p2g * k2[...].astype(F32) * conv[...].astype(F32)).astype(BF16)
    next_p = (edge[:, :BLK].astype(F32) + beside[...]).astype(BF16)
    near = (next_p.astype(F32) * edge[:, BLK:].astype(F32)).astype(BF16)
    last = lax.axis_index("ctx") == ctx_size - 1
    next_grad[...] = jnp.where(last, jnp.zeros(near.shape, BF16), near)
    for g in range(groups):
        kv, vv = rows_of(k1, g, size, 0, count).astype(F32), rows_of(v1, g, size, 0, count).astype(F32)
        here = rows_of(turned_grad, g, size, 0, count)
        after = jnp.concatenate([here[size:], next_grad[g * size : (g + 1) * size]], axis=0)
        p1g = dot(here, short[g, BLK:], 1, 1) + dot(after, short[g, 0:BLK], 1, 1)
        put_rows(k1_out, g, size, p1g * vv)
        put_rows(v1_out, g, size, p1g * kv)


def last_kernel(scale, n_ctx, *refs):
    moved, parts, (weight_out, filter_out, mixed) = refs[:n_ctx], refs[n_ctx:-3], refs[-3:]
    rows = weight_out.shape[1]
    me = lax.axis_index("ctx")
    total = None
    for k in range(n_ctx):
        weight_out[jnp.bitwise_xor(me, k)] = scale * moved[k][0:rows].astype(F32)
        term = unpack_rows(moved[k], rows, moved[k].shape[0] - rows, BLK)
        total = term if total is None else total + term
    filter_out[...] = scale * total
    summed = parts[0][...].astype(F32)
    for part in parts[1:]:
        summed = summed + part[...].astype(F32)
    mixed[...] = summed.astype(BF16)


def call(kernel, outs, *args, held=(), far=(), scratch=(), name):
    size = sum(math.prod(a.shape) * a.dtype.itemsize for a in args)
    size += sum(math.prod(s) * jnp.dtype(t).itemsize for s, t in outs)
    args = [pltpu.with_memory_space_constraint(a, pltpu.HBM) if i in far else a for i, a in enumerate(args)]
    results = pl.pallas_call(
        kernel,
        out_shape=[
            pltpu.VMEM(s, t) if i in held else pltpu.HBM(s, t) for i, (s, t) in enumerate(outs)
        ],
        in_specs=[
            pl.BlockSpec(memory_space=pltpu.HBM if name == "tables" and i > 2 else pltpu.VMEM)
            for i in range(len(args))
        ],
        out_specs=[pl.BlockSpec(memory_space=pltpu.VMEM)] * len(outs),
        scratch_shapes=list(scratch),
        cost_estimate=pl.CostEstimate(flops=0, bytes_accessed=size, transcendentals=0),
        compiler_params=pltpu.CompilerParams(vmem_limit_bytes=VMEM_LIMIT),
    )(*args)
    return [
        pltpu.with_memory_space_constraint(o, pltpu.VMEM) if i in held else o
        for i, o in enumerate(results)
    ]


def around(count, step):
    return [(i, (i + step) % count) for i in range(count)]


def exchange(blocks, count):
    out = [blocks[0]]
    for i in range(1, count // 2):
        out.append(lax.ppermute(blocks[i], "ctx", [(d, d ^ (2 * i)) for d in range(count)]))
    return out


def gather(block, count):
    out = {0: block}
    for k in [1] + list(range(2, count, 2)):
        out[k] = lax.ppermute(block, "ctx", [(i, i ^ k) for i in range(count)])
    for k in range(2, count, 2):
        out[k + 1] = lax.ppermute(out[k], "ctx", [(i, i ^ 1) for i in range(count)])
    return [out[k] for k in range(count)]


def on_device(q1, k1, v1, q2, k2, out_grad, taps, rate, residue, weight):
    chans, length = q1.shape
    groups, _ = taps.shape
    modes = rate.shape[1]
    size = chans // groups
    half = groups * modes
    count = length // BLK
    n_ctx, n_ch = lax.axis_size("ctx"), lax.axis_size("ch")
    rows = chans // n_ctx
    fused = rows % 16 == 0 and groups == modes == 16 and 4 * chans == weight.shape[1]
    fused = fused and n_ctx & (n_ctx - 1) == 0
    out_chans = weight.shape[1]
    width = out_chans // n_ch

    tail = (k1[:, length - BLK :].astype(F32) * v1[:, length - BLK :].astype(F32)).astype(BF16)
    halo = lax.ppermute(tail, "ctx", around(n_ctx, 1))
    grads = []
    for k in range(1, n_ch):
        grads.append(lax.ppermute(out_grad, "ch", around(n_ch, k)))

    coef = residue * jnp.sqrt(-jnp.expm1(-2.0 * rate))
    loaded = [
        pltpu.with_memory_space_constraint(a, pltpu.HBM)
        for a in (q1, k1, v1, q2, k2, out_grad, weight)
    ]
    late_q1, late_k1, late_v1, _, late_k2 = loaded[:5]
    short, long, close, open_, reach, rate_t, coef_t, q1, k1, v1, q2, k2, out_grad, weight = call(
        functools.partial(tables_kernel, size, len(loaded)),
        [
            ((groups, 2 * BLK, BLK), BF16),
            ((groups, BLK, BLK), BF16),
            ((2 * half, BLK), BF16),
            ((2 * half, BLK), BF16),
            ((3 * half, BLK), BF16),
            ((modes, chans), F32),
            ((modes, chans), F32),
        ]
        + [(a.shape, a.dtype) for a in loaded],
        taps,
        rate,
        coef,
        *loaded,
        held=range(14),
        scratch=[pltpu.SemaphoreType.DMA((len(loaded),))],
        name="tables",
    )
    stream = ((chans, length), BF16)
    blocks = ((count, modes, chans), F32)
    conv, gated, local, mirrored, ahead, sub, sent = call(
        functools.partial(first_kernel, size),
        [stream] * 3
        + [
            ((chans, length + BLK), BF16),
            ((chans, BLK), BF16),
            blocks,
            ((n_ctx, modes, chans), F32),
        ],
        halo,
        q1,
        k1,
        v1,
        k2,
        short,
        long,
        close,
        rate_t,
        held=(2, 3, 5, 6),
        scratch=[pltpu.VMEM((chans, length), BF16)],
        name="first",
    )
    states = lax.all_to_all(sent, "ctx", 0, 0, tiled=True)
    conv2, gated2, *parts = call(
        functools.partial(second_kernel, size, groups),
        [stream] * 2 + [((width, length), BF16)] * n_ch,
        states,
        sub,
        rate_t,
        coef_t,
        reach,
        local,
        q2,
        weight,
        held=range(2),
        name="second",
    )
    mixed_parts = [parts[0]]
    for k in range(1, n_ch):
        mixed_parts.append(lax.ppermute(parts[k], "ch", around(n_ch, k)))
    packed = ((rows + modes // 2, out_chans), BF16)
    if fused:
        sent_shapes = [
            ((chans // 2, out_chans), BF16),
            ((chans // 2 + modes // 2, out_chans), BF16),
            ((modes // 2, out_chans), BF16),
        ]
    else:
        sent_shapes = [((n_ctx, modes, chans), F32), ((chans, out_chans), F32)]
    q2_grad, local_back, sub_back, first_back, *sent_back = call(
        functools.partial(third_kernel, size, n_ch, n_ctx, fused),
        [stream] * 2 + [blocks, ((chans, BLK), BF16)] + sent_shapes,
        out_grad,
        *grads,
        weight,
        q2,
        conv2,
        gated2,
        long,
        open_,
        rate_t,
        scratch=[pltpu.VMEM((chans, out_chans), BF16), pltpu.VMEM((chans, length), BF16)],
        name="third",
    )
    edge_args = (first_back, sub_back, rate_t, coef_t, rate, ahead)
    edge_shape = ((chans, 2 * BLK), BF16)
    if fused:
        kept, crossing, own = sent_back
        got = lax.ppermute(crossing, "ctx", [(i, i ^ 1) for i in range(n_ctx)])
        edge, *blocks_back = call(
            functools.partial(pair_kernel, size),
            [edge_shape] + [((rows + modes, out_chans), BF16)] * (n_ctx // 2),
            kept,
            own,
            got,
            *edge_args,
            far=(0, 1, 3, 4, 8),
            name="pair",
        )
        states_back = exchange(blocks_back, n_ctx)
    else:
        states_back = [lax.all_to_all(sent_back[0], "ctx", 0, 0, tiled=True)]
        (edge,) = call(
            functools.partial(between_kernel, size),
            [edge_shape],
            *edge_args,
            far=(0, 1, 5),
            name="between",
        )
    next_edge = lax.ppermute(edge, "ctx", around(n_ctx, -1))
    beside, p2_grad, turned_grad, last = call(
        functools.partial(fourth_kernel, size, fused, n_ctx),
        [((chans, BLK), F32), stream, stream, packed if fused else ((groups, BLK), F32)],
        *states_back,
        sub_back,
        rate_t,
        coef_t,
        rate,
        local_back,
        late_q1,
        late_k2,
        mirrored,
        far=(0, n_ctx // 2) if fused else (),
        name="fourth",
    )
    scale = 1.0 / math.sqrt(length * n_ctx)
    if fused:
        final = gather(last, n_ctx)
    else:
        weight_total, filter_total = lax.psum((sent_back[1], last), "ctx")
    q2_out, k2_out, q1_out, k1_out, v1_out = call(
        functools.partial(fifth_kernel, size, n_ctx),
        [stream] * 5,
        p2_grad,
        turned_grad,
        beside,
        next_edge,
        q2_grad,
        gated,
        conv,
        late_k2,
        late_k1,
        late_v1,
        short,
        far=(0, 1, 2, 4, 5, 6),
        scratch=[pltpu.VMEM((chans, BLK), BF16)],
        name="fifth",
    )
    if fused:
        weight_grad, filter_grad, mixed = call(
            functools.partial(last_kernel, scale, n_ctx),
            [((n_ctx, rows, out_chans), F32), ((groups, BLK), F32), ((width, length), BF16)],
            *final,
            *mixed_parts,
            name="last",
        )
        weight_grad = weight_grad.reshape(chans, out_chans)
    else:
        weight_grad = scale * weight_total
        mixed = sum(p.astype(F32) for p in mixed_parts).astype(BF16)
        filter_grad = scale * filter_total
    return (mixed, q1_out, k1_out, v1_out, q2_out, k2_out, weight_grad, filter_grad)


def solution(mesh):
    cut, rows_only = P("ch", "ctx"), P("ch", None)

    return jax.shard_map(
        on_device,
        mesh=mesh,
        in_specs=(cut,) * 6 + (rows_only,) * 4,
        out_specs=(cut,) * 6 + (rows_only,) * 2,
        check_vma=False,
    )
```

```python
import functools
import math

import jax
import jax.numpy as jnp
from jax import lax
from jax.experimental import pallas as pl
from jax.experimental.pallas import tpu as pltpu
from jax.sharding import PartitionSpec as P

BLK = 128
VMEM_LIMIT = 12 << 20
PARTS = 2
HIGHEST = lax.Precision.HIGHEST
F32 = jnp.float32
BF16 = jnp.bfloat16


def dot(a, b, ca=1, cb=0, precision=None):
    return lax.dot_general(
        a, b, (((ca,), (cb,)), ((), ())), preferred_element_type=F32, precision=precision
    )


def split(x):
    hi = x.astype(BF16)
    return hi, (x - hi.astype(F32)).astype(BF16)


def iota(shape, dim):
    return lax.broadcasted_iota(jnp.int32, shape, dim)


def rows_of(ref, g, size, first, count):
    return jnp.concatenate(
        [
            ref[g * size : (g + 1) * size, (first + b) * BLK : (first + b + 1) * BLK]
            for b in range(count)
        ],
        axis=0,
    )


def put_rows(ref, g, size, value):
    for b in range(value.shape[0] // size):
        ref[g * size : (g + 1) * size, b * BLK : (b + 1) * BLK] = value[
            b * size : (b + 1) * size
        ].astype(ref.dtype)


def circulant(row):
    return pltpu.roll(jnp.broadcast_to(row, (BLK, BLK)), 0, 1, stride=1, stride_axis=0)


def column(table):
    groups, modes = table.shape
    wide = jnp.broadcast_to(table[:, None, :], (groups, modes, modes)).reshape(-1, modes)
    diag = iota(wide.shape, 0) % modes == iota(wide.shape, 1)
    return jnp.sum(jnp.where(diag, wide, 0.0), axis=1, keepdims=True)


def meeting(rate, groups, modes):
    half = groups * modes
    hi, lo = split(jnp.exp(-column(rate) * (BLK - iota((half, BLK), 1).astype(F32))))
    return jnp.concatenate([hi, hi, lo], axis=0)


def per_channel(table, size):
    groups = table.shape[0]
    chans = groups * size
    pick = (iota((groups, chans), 1) // size == iota((groups, chans), 0)).astype(F32)
    return dot(table, pick, 0, 0, HIGHEST)


def block_states(table, stream, groups, modes, size):
    half = groups * modes
    chans = groups * size
    full = dot(table, stream, 1, 1)
    full = full[:half] + full[half:]
    own = iota((half, chans), 0) // modes == iota((half, chans), 1) // size
    return jnp.sum(jnp.where(own, full, 0.0).reshape(groups, modes, chans), axis=0)


def state_terms(states, table, groups, modes, size):
    chans = groups * size
    half = groups * modes
    count = len(states)
    hi, lo = split(jnp.concatenate(states, axis=1))
    pick = (iota((modes, half), 1) % modes == iota((modes, half), 0)).astype(BF16)
    own = (iota((count * chans, half), 0) % chans) // size == iota((count * chans, half), 1) // modes
    wide_hi = jnp.where(own, dot(hi, pick, 0, 0), 0.0).astype(BF16)
    wide_lo = jnp.where(own, dot(lo, pick, 0, 0), 0.0).astype(BF16)
    out = dot(jnp.concatenate([wide_hi, wide_lo, wide_hi], axis=1), table)
    return [out[i * chans : (i + 1) * chans] for i in range(count)]


def pack_rows(ref, first, value):
    half, chans = value.shape[0] // 2, value.shape[1]
    for i, part in enumerate(split(value)):
        for j in range(2):
            at = (2 * i + j) * chans
            ref[first : first + half, at : at + chans] = part[j * half : (j + 1) * half]
    width = ref.shape[1]
    if 4 * chans < width:
        ref[first : first + half, 4 * chans :] = jnp.zeros((half, width - 4 * chans), BF16)


def unpack_rows(ref, first, half, chans):
    parts = [ref[first : first + half, i * chans : (i + 1) * chans].astype(F32) for i in range(4)]
    return jnp.concatenate([parts[0] + parts[2], parts[1] + parts[3]], axis=0)


def tables_kernel(size, held, *refs):
    taps, rate, coef = refs[:3]
    sources = refs[3 : 3 + held]
    (short, long, close, open_, reach, rate_t, coef_t) = refs[3 + held : 10 + held]
    targets, sems = refs[10 + held : -1], refs[-1]
    copies = [
        pltpu.make_async_copy(source, target, sems.at[i])
        for i, (source, target) in enumerate(zip(sources, targets))
    ]
    for copy in copies:
        copy.start()
    groups, modes = rate.shape
    half = groups * modes
    col, coef_col = column(rate[...]), column(coef[...])
    at = iota((half, BLK), 1).astype(F32)
    falling = jnp.exp(-col * at)
    hi, lo = split(falling)
    open_[0:half] = hi
    open_[half:] = lo
    hi, lo = split(jnp.exp(-col * (BLK - 1.0 - at)))
    close[0:half] = hi
    close[half:] = lo
    hi, lo = split(jnp.exp(-col * (at + 1.0)))
    reach[0:half] = hi
    reach[half : 2 * half] = hi
    reach[2 * half :] = lo
    kernel = jnp.sum((coef_col * falling).reshape(groups, modes, BLK), axis=1)
    tap_rows = taps[...].astype(F32)
    later = iota((BLK, BLK), 1) >= iota((BLK, BLK), 0)
    for g in range(groups):
        turned = circulant(tap_rows[g : g + 1])
        short[g, 0:BLK] = jnp.where(later, 0.0, turned).astype(BF16)
        short[g, BLK:] = jnp.where(later, turned, 0.0).astype(BF16)
        long[g] = jnp.where(later, circulant(kernel[g : g + 1]), 0.0).astype(BF16)
    rate_t[...] = per_channel(rate[...], size)
    coef_t[...] = per_channel(coef[...], size)
    for copy in copies:
        copy.wait()


def first_kernel(
    size,
    halo,
    q1,
    k1,
    v1,
    k2,
    short,
    long,
    close,
    rate_t,
    conv,
    gated,
    local,
    mirrored,
    ahead,
    sub,
    sent,
    stream,
):
    groups = short.shape[0]
    modes = rate_t.shape[0]
    count = q1.shape[1] // BLK
    seen = jnp.where(lax.axis_index("ctx") > 0, halo[...], jnp.zeros(halo.shape, BF16))
    mirror = (iota((BLK, BLK), 1) + iota((BLK, BLK), 0) == BLK - 1).astype(BF16)
    for g in range(groups):
        rows = slice(g * size, (g + 1) * size)
        p1 = (rows_of(k1, g, size, 0, count).astype(F32) * rows_of(v1, g, size, 0, count).astype(F32)).astype(BF16)
        before = jnp.concatenate([seen[rows], p1[: (count - 1) * size]], axis=0)
        c1 = dot(jnp.concatenate([before, p1], axis=1), short[g])
        put_rows(conv, g, size, c1)
        g1 = (rows_of(q1, g, size, 0, count).astype(F32) * c1).astype(BF16)
        put_rows(gated, g, size, g1)
        p2 = (rows_of(k2, g, size, 0, count).astype(F32) * g1.astype(F32)).astype(BF16)
        put_rows(stream, g, size, p2)
        put_rows(local, g, size, dot(p2, long[g]))
    mirrored[:, :BLK] = dot(seen, mirror).astype(BF16)
    ahead[...] = (k2[:, :BLK].astype(F32) * q1[:, :BLK].astype(F32)).astype(BF16)
    for b in range(count):
        cols = slice(b * BLK, (b + 1) * BLK)
        p1 = (k1[:, cols].astype(F32) * v1[:, cols].astype(F32)).astype(BF16)
        mirrored[:, (b + 1) * BLK : (b + 2) * BLK] = dot(p1, mirror).astype(BF16)
    decay = jnp.exp(-rate_t[...] * BLK)
    total = None
    for b in range(count):
        state = block_states(close[...], stream[:, b * BLK : (b + 1) * BLK], groups, modes, size)
        sub[b] = state
        total = state if total is None else total * decay + state
    for d in range(sent.shape[0]):
        sent[d] = total


def second_kernel(
    size, groups, states, sub, rate_t, coef_t, reach, local, q2, weight, conv2, gated2, *parts
):
    modes = rate_t.shape[0]
    ctx_size, count = states.shape[0], sub.shape[0]
    length = float(count * BLK)
    me = lax.axis_index("ctx")
    rate = rate_t[...]
    entering = jnp.zeros(rate.shape, F32)
    for d in range(ctx_size):
        gap = me - 1 - d
        factor = jnp.exp(-rate * (length * jnp.maximum(gap, 0).astype(F32)))
        entering = entering + jnp.where(gap >= 0, factor * states[d], 0.0)
    decay = jnp.exp(-rate * BLK)
    coefs = coef_t[...]
    all_states = []
    for b in range(count):
        all_states.append(coefs * entering)
        entering = decay * entering + sub[b]
    terms = state_terms(all_states, reach[...], groups, modes, size)
    for b in range(count):
        cols = slice(b * BLK, (b + 1) * BLK)
        c2 = (local[:, cols].astype(F32) + terms[b]).astype(BF16)
        conv2[:, cols] = c2
        gated2[:, cols] = (q2[:, cols].astype(F32) * c2.astype(F32)).astype(BF16)
    here = lax.axis_index("ch")
    width = weight.shape[1] // len(parts)
    for k, part in enumerate(parts):
        at = pl.multiple_of(lax.rem(here + k, len(parts)) * width, BLK)
        part[...] = dot(weight[:, pl.ds(at, width)], gated2[...], 0, 0).astype(BF16)


def third_kernel(size, n_ch, n_ctx, fused, *refs):
    grads = refs[:n_ch]
    (weight, q2, conv2, gated2, long, open_, rate_t) = refs[n_ch : n_ch + 7]
    (q2_grad, local, sub, first, *sent) = refs[n_ch + 7 : -2]
    whole, stream = refs[-2:]
    groups = long.shape[0]
    modes, chans = rate_t.shape
    count = q2.shape[1] // BLK
    here = lax.axis_index("ch")
    width = weight.shape[1] // n_ch
    starts = [
        pl.multiple_of(lax.rem(here - k + n_ch, n_ch) * width, BLK) for k in range(n_ch)
    ]
    acc = None
    for k in range(n_ch):
        term = dot(weight[:, pl.ds(starts[k], width)], grads[k][...])
        acc = term if acc is None else acc + term
    q2_grad[...] = (acc * conv2[...].astype(F32)).astype(BF16)
    stream[...] = (acc * q2[...].astype(F32)).astype(BF16)
    for g in range(groups):
        put_rows(local, g, size, dot(rows_of(stream, g, size, 0, count), long[g], 1, 1))
    decay = jnp.exp(-rate_t[...] * BLK)
    total = None
    for b in reversed(range(count)):
        state = block_states(open_[...], stream[:, b * BLK : (b + 1) * BLK], groups, modes, size)
        sub[b] = state
        total = state if total is None else total * decay + state
    first[...] = local[:, :BLK]
    for k in range(n_ch):
        part = dot(gated2[...], grads[k][...], 1, 1)
        if fused:
            whole[:, pl.ds(starts[k], width)] = part.astype(BF16)
        else:
            sent[1][:, pl.ds(starts[k], width)] = part
    if fused:
        rows = chans // n_ctx
        me = lax.axis_index("ctx")
        for i in range(n_ctx // 2):
            for j in range(2):
                at = pl.multiple_of(jnp.bitwise_xor(me, 2 * i + j) * rows, rows)
                sent[j][i * rows : (i + 1) * rows] = whole[pl.ds(at, rows), :]
        pack_rows(sent[1], n_ctx // 2 * rows, total)
        pack_rows(sent[2], 0, total)
    else:
        for d in range(n_ctx):
            sent[0][d] = total


def pair_kernel(size, kept, own, got, local, sub, rate_t, coef_t, rate_g, ahead, edge, *out):
    half = own.shape[0]
    rows = kept.shape[0] // len(out)
    for i, block in enumerate(out):
        at = slice(i * rows, (i + 1) * rows)
        block[0:rows] = (kept[at].astype(F32) + got[at].astype(F32)).astype(BF16)
        block[rows : rows + half] = own[...]
        block[rows + half :] = got[len(out) * rows :]
    between_kernel(size, local, sub, rate_t, coef_t, rate_g, ahead, edge)


def between_kernel(size, local, sub, rate_t, coef_t, rate_g, ahead, edge):
    modes, chans = rate_t.shape
    count = sub.shape[0]
    decay = jnp.exp(-rate_t[...] * BLK)
    inner = sub[count - 1]
    for b in reversed(range(1, count - 1)):
        inner = inner * decay + sub[b]
    meet = meeting(rate_g[...], chans // size, modes)
    (term,) = state_terms([coef_t[...] * inner], meet, chans // size, modes, size)
    edge[:, :BLK] = (local[...].astype(F32) + term).astype(BF16)
    edge[:, BLK:] = ahead[...]


def fourth_kernel(size, fused, n_ctx, *refs):
    moved = refs[: n_ctx // 2 if fused else 1]
    (sub, rate_t, coef_t, rate_g, local, q1, k2, mirrored) = refs[len(moved) : len(moved) + 8]
    (beside, p2_grad, turned_grad, out) = refs[len(moved) + 8 :]
    modes, chans = rate_t.shape
    groups = chans // size
    count = sub.shape[0]
    length = float(count * BLK)
    rows = chans // n_ctx
    me = lax.axis_index("ctx")
    rate = rate_t[...]
    coefs = coef_t[...]
    beyond = jnp.zeros(rate.shape, F32)
    following = jnp.zeros(rate.shape, F32)
    for k in range(n_ctx):
        if fused:
            at = rows + k % 2 * (modes // 2)
            state = unpack_rows(moved[k // 2], at, modes // 2, chans)
        else:
            state = moved[0][k]
        gap = (jnp.bitwise_xor(me, k) if fused else k) - me - 2
        factor = jnp.exp(-rate * (length * jnp.maximum(gap, 0).astype(F32)))
        beyond = beyond + jnp.where(gap >= 0, factor * state, 0.0)
        following = following + jnp.where(gap == -1, state, 0.0)
    decay = jnp.exp(-rate * BLK)
    entering = jnp.exp(-rate * length) * beyond + following
    all_states = [coefs * (jnp.exp(-rate * (length - BLK)) * beyond)]
    for b in reversed(range(count)):
        all_states.append(coefs * entering)
        entering = decay * entering + sub[b]
    terms = state_terms(all_states, meeting(rate_g[...], groups, modes), groups, modes, size)
    beside[...] = terms[0]
    for b in range(count):
        cols = slice(b * BLK, (b + 1) * BLK)
        p2g = (local[:, cols].astype(F32) + terms[count - b]).astype(BF16)
        p2_grad[:, cols] = p2g
        g1g = p2g.astype(F32) * k2[:, cols].astype(F32)
        turned_grad[:, cols] = (g1g * q1[:, cols].astype(F32)).astype(BF16)
    later = iota((BLK, BLK), 1) + iota((BLK, BLK), 0) >= BLK - 1
    filters = []
    for g in range(groups):
        here = rows_of(turned_grad, g, size, 0, count)
        seen = rows_of(mirrored, g, size, 0, count + 1)
        inside = dot(seen[size:], here, 0, 0)
        across = dot(seen[: count * size], here, 0, 0)
        turned = pltpu.roll(jnp.where(later, inside, across), 1, 1, stride=1, stride_axis=0)
        filters.append(jnp.sum(turned, axis=0, keepdims=True))
    filter_rows = jnp.concatenate(filters, axis=0)
    if fused:
        total = moved[0][0:rows].astype(F32)
        for block in moved[1:]:
            total = total + block[0:rows].astype(F32)
        out[0:rows] = total.astype(BF16)
        pack_rows(out, rows, filter_rows)
    else:
        out[...] = filter_rows


def fifth_kernel(size, ctx_size, p2_grad, turned_grad, beside, edge, gated, conv, k2, k1, v1, short, k2_out, q1_out, k1_out, v1_out, next_grad):
    groups = short.shape[0]
    count = p2_grad.shape[1] // BLK
    p2g = p2_grad[...].astype(F32)
    k2_out[...] = (p2g * gated[...].astype(F32)).astype(BF16)
    q1_out[...] = (p2g * k2[...].astype(F32) * conv[...].astype(F32)).astype(BF16)
    next_p = (edge[:, :BLK].astype(F32) + beside[...]).astype(BF16)
    near = (next_p.astype(F32) * edge[:, BLK:].astype(F32)).astype(BF16)
    last = lax.axis_index("ctx") == ctx_size - 1
    next_grad[...] = jnp.where(last, jnp.zeros(near.shape, BF16), near)
    for g in range(groups):
        kv, vv = rows_of(k1, g, size, 0, count).astype(F32), rows_of(v1, g, size, 0, count).astype(F32)
        here = rows_of(turned_grad, g, size, 0, count)
        after = jnp.concatenate([here[size:], next_grad[g * size : (g + 1) * size]], axis=0)
        p1g = dot(here, short[g, BLK:], 1, 1) + dot(after, short[g, 0:BLK], 1, 1)
        put_rows(k1_out, g, size, p1g * vv)
        put_rows(v1_out, g, size, p1g * kv)


def last_kernel(scale, n_ctx, *refs):
    moved, parts, (weight_out, filter_out, mixed) = refs[:n_ctx], refs[n_ctx:-3], refs[-3:]
    rows = weight_out.shape[1]
    me = lax.axis_index("ctx")
    total = None
    for k in range(n_ctx):
        weight_out[jnp.bitwise_xor(me, k)] = scale * moved[k][0:rows].astype(F32)
        term = unpack_rows(moved[k], rows, moved[k].shape[0] - rows, BLK)
        total = term if total is None else total + term
    filter_out[...] = scale * total
    summed = parts[0][...].astype(F32)
    for part in parts[1:]:
        summed = summed + part[...].astype(F32)
    mixed[...] = summed.astype(BF16)


def call(kernel, outs, *args, held=(), far=(), scratch=(), parts=1, name):
    size = sum(math.prod(a.shape) * a.dtype.itemsize for a in args)
    size += sum(math.prod(s) * jnp.dtype(t).itemsize for s, t in outs)
    args = [pltpu.with_memory_space_constraint(a, pltpu.HBM) if i in far else a for i, a in enumerate(args)]
    if parts > 1:
        def cut(shape):
            rest = len(shape) - 1
            return pl.BlockSpec((shape[0] // parts, *shape[1:]), lambda i: (i,) + (0,) * rest)

        extra = dict(grid=(parts,))
        in_specs = [cut(a.shape) for a in args]
        out_specs = [cut(s) for s, t in outs]
    else:
        extra = {}
        in_specs = [
            pl.BlockSpec(memory_space=pltpu.HBM if name == "tables" and i > 2 else pltpu.VMEM)
            for i in range(len(args))
        ]
        out_specs = [pl.BlockSpec(memory_space=pltpu.VMEM)] * len(outs)
    results = pl.pallas_call(
        kernel,
        out_shape=[
            pltpu.VMEM(s, t) if i in held else pltpu.HBM(s, t) for i, (s, t) in enumerate(outs)
        ],
        in_specs=in_specs,
        out_specs=out_specs,
        **extra,
        scratch_shapes=list(scratch),
        cost_estimate=pl.CostEstimate(flops=0, bytes_accessed=size, transcendentals=0),
        compiler_params=pltpu.CompilerParams(vmem_limit_bytes=VMEM_LIMIT),
    )(*args)
    return [
        pltpu.with_memory_space_constraint(o, pltpu.VMEM) if i in held else o
        for i, o in enumerate(results)
    ]


def around(count, step):
    return [(i, (i + step) % count) for i in range(count)]


def exchange(blocks, count):
    out = [blocks[0]]
    for i in range(1, count // 2):
        out.append(lax.ppermute(blocks[i], "ctx", [(d, d ^ (2 * i)) for d in range(count)]))
    return out


def gather(block, count):
    out = {0: block}
    for k in [1] + list(range(2, count, 2)):
        out[k] = lax.ppermute(block, "ctx", [(i, i ^ k) for i in range(count)])
    for k in range(2, count, 2):
        out[k + 1] = lax.ppermute(out[k], "ctx", [(i, i ^ 1) for i in range(count)])
    return [out[k] for k in range(count)]


def on_device(q1, k1, v1, q2, k2, out_grad, taps, rate, residue, weight):
    chans, length = q1.shape
    groups, _ = taps.shape
    modes = rate.shape[1]
    size = chans // groups
    half = groups * modes
    count = length // BLK
    n_ctx, n_ch = lax.axis_size("ctx"), lax.axis_size("ch")
    rows = chans // n_ctx
    fused = rows % 16 == 0 and groups == modes == 16 and 4 * chans == weight.shape[1]
    fused = fused and n_ctx & (n_ctx - 1) == 0
    out_chans = weight.shape[1]
    width = out_chans // n_ch

    tail = (k1[:, length - BLK :].astype(F32) * v1[:, length - BLK :].astype(F32)).astype(BF16)
    halo = lax.ppermute(tail, "ctx", around(n_ctx, 1))
    grads = []
    for k in range(1, n_ch):
        grads.append(lax.ppermute(out_grad, "ch", around(n_ch, k)))

    coef = residue * jnp.sqrt(-jnp.expm1(-2.0 * rate))
    loaded = [
        pltpu.with_memory_space_constraint(a, pltpu.HBM)
        for a in (q1, k1, v1, q2, k2, out_grad, weight)
    ]
    late_q1, late_k1, late_v1, _, late_k2 = loaded[:5]
    short, long, close, open_, reach, rate_t, coef_t, q1, k1, v1, q2, k2, out_grad, weight = call(
        functools.partial(tables_kernel, size, len(loaded)),
        [
            ((groups, 2 * BLK, BLK), BF16),
            ((groups, BLK, BLK), BF16),
            ((2 * half, BLK), BF16),
            ((2 * half, BLK), BF16),
            ((3 * half, BLK), BF16),
            ((modes, chans), F32),
            ((modes, chans), F32),
        ]
        + [(a.shape, a.dtype) for a in loaded],
        taps,
        rate,
        coef,
        *loaded,
        held=range(14),
        scratch=[pltpu.SemaphoreType.DMA((len(loaded),))],
        name="tables",
    )
    stream = ((chans, length), BF16)
    blocks = ((count, modes, chans), F32)
    conv, gated, local, mirrored, ahead, sub, sent = call(
        functools.partial(first_kernel, size),
        [stream] * 3
        + [
            ((chans, length + BLK), BF16),
            ((chans, BLK), BF16),
            blocks,
            ((n_ctx, modes, chans), F32),
        ],
        halo,
        q1,
        k1,
        v1,
        k2,
        short,
        long,
        close,
        rate_t,
        held=(2, 5, 6),
        scratch=[pltpu.VMEM((chans, length), BF16)],
        name="first",
    )
    states = lax.all_to_all(sent, "ctx", 0, 0, tiled=True)
    conv2, gated2, *parts = call(
        functools.partial(second_kernel, size, groups),
        [stream] * 2 + [((width, length), BF16)] * n_ch,
        states,
        sub,
        rate_t,
        coef_t,
        reach,
        local,
        q2,
        weight,
        held=range(2),
        name="second",
    )
    mixed_parts = [parts[0]]
    for k in range(1, n_ch):
        mixed_parts.append(lax.ppermute(parts[k], "ch", around(n_ch, k)))
    packed = ((rows + modes // 2, out_chans), BF16)
    if fused:
        sent_shapes = [
            ((chans // 2, out_chans), BF16),
            ((chans // 2 + modes // 2, out_chans), BF16),
            ((modes // 2, out_chans), BF16),
        ]
    else:
        sent_shapes = [((n_ctx, modes, chans), F32), ((chans, out_chans), F32)]
    q2_grad, local_back, sub_back, first_back, *sent_back = call(
        functools.partial(third_kernel, size, n_ch, n_ctx, fused),
        [stream] * 2 + [blocks, ((chans, BLK), BF16)] + sent_shapes,
        out_grad,
        *grads,
        weight,
        q2,
        conv2,
        gated2,
        long,
        open_,
        rate_t,
        scratch=[pltpu.VMEM((chans, out_chans), BF16), pltpu.VMEM((chans, length), BF16)],
        name="third",
    )
    edge_args = (first_back, sub_back, rate_t, coef_t, rate, ahead)
    edge_shape = ((chans, 2 * BLK), BF16)
    if fused:
        kept, crossing, own = sent_back
        got = lax.ppermute(crossing, "ctx", [(i, i ^ 1) for i in range(n_ctx)])
        edge, *blocks_back = call(
            functools.partial(pair_kernel, size),
            [edge_shape] + [((rows + modes, out_chans), BF16)] * (n_ctx // 2),
            kept,
            own,
            got,
            *edge_args,
            far=(0, 1, 3, 4, 8),
            name="pair",
        )
        states_back = exchange(blocks_back, n_ctx)
    else:
        states_back = [lax.all_to_all(sent_back[0], "ctx", 0, 0, tiled=True)]
        (edge,) = call(
            functools.partial(between_kernel, size),
            [edge_shape],
            *edge_args,
            far=(0, 1, 5),
            name="between",
        )
    next_edge = lax.ppermute(edge, "ctx", around(n_ctx, -1))
    beside, p2_grad, turned_grad, last = call(
        functools.partial(fourth_kernel, size, fused, n_ctx),
        [((chans, BLK), F32), stream, stream, packed if fused else ((groups, BLK), F32)],
        *states_back,
        sub_back,
        rate_t,
        coef_t,
        rate,
        local_back,
        late_q1,
        late_k2,
        mirrored,
        far=(0, n_ctx // 2, n_ctx // 2 + 7) if fused else (),
        name="fourth",
    )
    scale = 1.0 / math.sqrt(length * n_ctx)
    if fused:
        final = gather(last, n_ctx)
    else:
        weight_total, filter_total = lax.psum((sent_back[1], last), "ctx")
    k2_out, q1_out, k1_out, v1_out = call(
        functools.partial(fifth_kernel, size, n_ctx),
        [stream] * 4,
        p2_grad,
        turned_grad,
        beside,
        next_edge,
        gated,
        conv,
        late_k2,
        late_k1,
        late_v1,
        short,
        far=(0, 1, 2, 4, 5),
        scratch=[pltpu.VMEM((chans // PARTS, BLK), BF16)],
        parts=PARTS,
        name="fifth",
    )
    if fused:
        weight_grad, filter_grad, mixed = call(
            functools.partial(last_kernel, scale, n_ctx),
            [((n_ctx, rows, out_chans), F32), ((groups, BLK), F32), ((width, length), BF16)],
            *final,
            *mixed_parts,
            name="last",
        )
        weight_grad = weight_grad.reshape(chans, out_chans)
    else:
        weight_grad = scale * weight_total
        mixed = sum(p.astype(F32) for p in mixed_parts).astype(BF16)
        filter_grad = scale * filter_total
    return (mixed, q1_out, k1_out, v1_out, q2_grad, k2_out, weight_grad, filter_grad)


def solution(mesh):
    cut, rows_only = P("ch", "ctx"), P("ch", None)

    return jax.shard_map(
        on_device,
        mesh=mesh,
        in_specs=(cut,) * 6 + (rows_only,) * 4,
        out_specs=(cut,) * 6 + (rows_only,) * 2,
        check_vma=False,
    )
```
